128 devices in a mesh: lon: 32 (over y, z, core), lat: 4 (over x).
Axes of the slice: x: 4, y: 4, z: 4, core: 2. Of those that a mesh axis runs over, the one named last changes fastest.
Arguments:
- spectra: float32 [25, 36, 131072], P(None, None, ('lon', 'lat')), may hold values from 0 to 1
- wind_growth: float32 [131072], P(('lon', 'lat')), may hold values from 0.05 to 0.6
- wind_dir: float32 [131072], P(('lon', 'lat')), may hold values from -3.140625 to 3.140625
- point_cell: int32 [131072], P(('lon', 'lat')), may hold values from -1 to 131071, as said below
- land_mask: int32 [64, 2048], P('lon', 'lat'), may hold values from 0 to 1, as said below
- shoaling: float32 [64, 2048], P('lon', 'lat'), may hold values from 0.5 to 1
- slope_x: float32 [64, 2048], P('lon', 'lat'), may hold values from -0.5 to 0.5
- slope_y: float32 [64, 2048], P('lon', 'lat'), may hold values from -0.5 to 0.5
Outputs:
- wave_field: float32 [25, 36, 64, 2048], P(None, None, 'lon', 'lat')
The draws below stay inside these ranges and needn't reach their ends.
Inputs may be any that keep to these rules, and one draw needn't show every extreme that they name: `point_cell`: every sea cell of land_mask is named by exactly one slot over all devices, land cells by none, other slots hold -1. The slots of one device name at most 8 cells of any one device's block of 2 x 512 cells, and in every draw some block gets exactly 8 from every device. `land_mask`: at least a quarter of the cells of each device's block are sea; some block is all sea.
All inputs are finite; a program needn't handle non-finite values.
Results may differ from the reference program's by a relative error of at most 0.0001.
Values sent between devices are 32-bit elements; how exact they have to be, the bound alone decides.
A program may use at most 128 MiB of HBM per device.

```python
import math
import jax
import jax.numpy as jnp
from jax import lax

NF = 25
ND = 36
GX = 2
GY = 512
NSUB = 2
NX = 64
NY = 2048
POINTS = 131072
N_LON = 32
N_LAT = 4


def build_layout(key):
    devices = N_LON * N_LAT
    cells = GX * GY
    key_rank, key_count, key_full, key_shift, key_slot = jax.random.split(jax.random.fold_in(key, 11), 5)
    ranks = jax.vmap(lambda k: jax.random.permutation(k, cells))(jax.random.split(key_rank, devices))
    counts = jax.random.randint(key_count, (devices,), cells // 4, cells + 1)
    full = jax.random.randint(key_full, (), 0, devices)
    counts = jnp.where(jnp.arange(devices) == full, cells, counts)
    tile = jnp.arange(devices)[:, None]
    local = jnp.arange(cells)[None, :]
    corner = (tile == devices - 1) & (local == cells - 1)
    sea = (ranks < counts[:, None]) | corner
    lon_id = tile // N_LAT
    lat_id = tile % N_LAT
    glob_x = lon_id * GX + local // GY
    glob_y = lat_id * GY + local % GY
    cell_id = (glob_x * (GY * N_LAT) + glob_y).astype(jnp.int32)
    shift = jax.random.randint(key_shift, (devices, 1), 0, devices)
    source = (ranks + shift) % devices
    canon = tile * (cells // devices) + ranks // devices
    flat_target = jnp.where(sea, source * cells + canon, devices * cells)
    holder = jnp.full((devices * cells,), -1, jnp.int32)
    holder = holder.at[flat_target.reshape(-1)].set(cell_id.reshape(-1), mode='drop').reshape(devices, cells)
    perms = jax.vmap(lambda k: jax.random.permutation(k, cells))(jax.random.split(key_slot, devices))
    inverse = jnp.argsort(perms, axis=1)
    shuffled = jnp.take_along_axis(holder, inverse, axis=1)
    return (sea, shuffled)


def draw_point_cell(key, part):
    sea, shuffled = build_layout(key)
    return shuffled.reshape(-1).astype(jnp.int32)


def draw_land_mask(key, part):
    sea, shuffled = build_layout(key)
    grid = sea.astype(jnp.int32).reshape(N_LON, N_LAT, GX, GY)
    return jnp.transpose(grid, (0, 2, 1, 3)).reshape(GX * N_LON, GY * N_LAT)


def draw_spectra(key, part):
    key_scale, key_entry = jax.random.split(jax.random.fold_in(key, 23), 2)
    total = GX * GY * N_LON * N_LAT
    scale = jnp.exp(jax.random.uniform(key_scale, (total,), jnp.float32, math.log(0.1), 0.0))
    entries = jax.random.uniform(key_entry, (NF, ND, total), jnp.float32, 0.1, 1.0)
    return (entries * scale[None, None, :]).astype(jnp.float32)


def levels(own_key, extent, cuts, least, largest):
    factor_of = 1.0
    for position, parts in cuts:
        heights = jax.random.uniform(jax.random.fold_in(jax.random.fold_in(own_key, 6), position), (parts,), jnp.float32, least / len(cuts), largest / len(cuts))
        factor_of = factor_of * jnp.repeat(jnp.exp(heights), extent[position] // parts).reshape((-1,) + (1,) * (len(extent) - 1 - position))
    return factor_of


def setup_inputs(seed: int = 0) -> dict:
    key_list = jax.random.split(jax.random.key(seed), 9)
    return {
        "spectra": draw_spectra(jax.random.fold_in(key_list[8], 71), 0),
        "wind_growth": jnp.clip(jnp.exp(math.log(0.6) - 2.4849067 * jax.random.uniform(key_list[1], (POINTS,), jnp.float32) ** levels(key_list[1], (POINTS,), ((0, 128),), -0.2, 0.2)), 0.05, 0.6),
        "wind_dir": jnp.clip(jax.random.uniform(key_list[2], (POINTS,), jnp.float32, -3.140625, 3.140625), -3.140625, 3.140625),
        "point_cell": draw_point_cell(jax.random.fold_in(key_list[8], 71), 0),
        "land_mask": draw_land_mask(jax.random.fold_in(key_list[8], 71), 0),
        "shoaling": jnp.clip(0.5 + 0.5 * jax.random.uniform(key_list[5], (NX, NY), jnp.float32) ** levels(key_list[5], (NX, NY), ((0, 32), (1, 4)), -0.2, 0.2), 0.5, 1.0),
        "slope_x": jnp.clip(jax.random.uniform(key_list[6], (NX, NY), jnp.float32, -0.5, 0.5) * levels(key_list[6], (NX, NY), ((0, 32), (1, 4)), -0.4, 0.0), -0.5, 0.5),
        "slope_y": jnp.clip(jax.random.uniform(key_list[7], (NX, NY), jnp.float32, -0.5, 0.5) * levels(key_list[7], (NX, NY), ((0, 32), (1, 4)), -0.4, 0.0), -0.5, 0.5),
    }


def spectral_tables(nfreq, ndir):
    level = jnp.arange(nfreq, dtype=jnp.float32)
    ratio = 1.1 ** (level - (nfreq - 1))
    speed = 0.65 * 1.1 ** (-level)
    width = 0.1 * 1.1 ** level
    theta = (jnp.arange(ndir, dtype=jnp.float32) + 0.5) * (2.0 * math.pi / ndir)
    return ratio, speed, width, theta


def propagate(field, speed_f, shoaling, slope_x, slope_y, sea, cos_t, sin_t):
    cx = speed_f * shoaling[None] * cos_t[:, None, None]
    cy = speed_f * shoaling[None] * sin_t[:, None, None]
    turn = speed_f * (sin_t[:, None, None] * slope_x[None] - cos_t[:, None, None] * slope_y[None])
    for step in range(NSUB):
        qx = cx * field
        qy = cy * field
        flux_x = jnp.maximum(qx, 0.0) + jnp.minimum(jnp.roll(qx, -1, axis=1), 0.0)
        net_x = flux_x - jnp.roll(flux_x, 1, axis=1)
        padq = jnp.pad(qy, ((0, 0), (0, 0), (1, 1)))
        flux_y = jnp.maximum(padq[:, :, :-1], 0.0) + jnp.minimum(padq[:, :, 1:], 0.0)
        net_y = flux_y[:, :, 1:] - flux_y[:, :, :-1]
        half = field - net_x - net_y
        qt = turn * half
        flux_t = jnp.maximum(qt, 0.0) + jnp.minimum(jnp.roll(qt, -1, axis=0), 0.0)
        field = (half - flux_t + jnp.roll(flux_t, 1, axis=0)) * sea
    return field


def reference(spectra, wind_growth, wind_dir, point_cell, land_mask, shoaling, slope_x, slope_y):
    ratio, speed, width, theta = spectral_tables(NF, ND)
    dtheta = 2.0 * math.pi / ND

    def accumulate(f, total):
        return total + width[f] * dtheta * jnp.sum(spectra[f], axis=0)

    energy = lax.fori_loop(0, NF, accumulate, jnp.zeros((POINTS,), jnp.float32))
    load = energy / (energy + 10.0)
    lobe = jnp.maximum(jnp.cos(theta[:, None] - wind_dir[None, :]), 0.0) ** 2
    target = jnp.where(point_cell >= 0, point_cell, NX * NY).astype(jnp.int32)
    sea = land_mask.astype(jnp.float32)
    cos_t = jnp.cos(theta)
    sin_t = jnp.sin(theta)

    def one_frequency(inputs):
        spec_f, speed_f, ratio_f = inputs
        rate = wind_growth[None, :] * lobe * ratio_f - 0.4 * ratio_f * load[None, :]
        sourced = spec_f * jnp.exp(rate)
        grid = jnp.zeros((ND, NX * NY + 1), jnp.float32).at[:, target].set(sourced)
        grid = grid[:, :NX * NY].reshape(ND, NX, NY)
        return propagate(grid, speed_f, shoaling, slope_x, slope_y, sea, cos_t, sin_t)

    return lax.map(one_frequency, (spectra, speed, ratio))
```

```python
import math

import jax
import jax.numpy as jnp
from jax import lax
from jax.experimental import pallas as pl
from jax.experimental.pallas import tpu as pltpu
from jax.sharding import PartitionSpec as P

MESH = pl.DeviceIdType.MESH
F32 = jnp.float32
BF16 = jnp.bfloat16

NF, ND = 25, 36
GX, GY = 2, 512
NLON, NLAT = 32, 4
NDEV = NLON * NLAT
CELLS = GX * GY
CAP = CELLS // NDEV
NT = 7
ROWS = 57
DTH = 2.0 * math.pi / ND
THETA = [(d + 0.5) * DTH for d in range(ND)]
COS = [math.cos(t) for t in THETA]
SIN = [math.sin(t) for t in THETA]
RATIO = [1.1 ** (f - (NF - 1)) for f in range(NF)]
WIDTH = [0.1 * 1.1**f * DTH for f in range(NF)]
CPLUS = [d for d in range(27, 36)] + [d for d in range(0, 9)]
CMINUS = [d for d in range(9, 27)]
SPLUS = list(range(0, 18))
SMINUS = list(range(18, 36))
PHALF = 9
VMEM_LIMIT = 60 << 20


def row_of(f, d):
    if f == NF - 1:
        return 36 * (NF - 1) + d
    base = 72 * (f // 2)
    if d < 32:
        return base + 32 * (f % 2) + d
    return base + 64 + 4 * (f % 2) + (d - 32)


def split(v):
    hi = v.astype(BF16)
    lo = (v - hi.astype(F32)).astype(BF16)
    return hi, lo


def nt_dot(a, b):
    return lax.dot_general(a, b, (((1,), (1,)), ((), ())), preferred_element_type=F32)


def nn_dot(a, b):
    return lax.dot_general(a, b, (((1,), (0,)), ((), ())), preferred_element_type=F32)


def source_kernel(spec_ref, wg_ref, wd_ref, pc_ref, out_ref, r_ref, v_ref, oh_ref, b_ref):
    wide = (1, CELLS)
    acc = jnp.zeros((8, CELLS), F32)
    acc4 = jnp.zeros((4, CELLS), F32)
    for f in range(NF):
        s = spec_ref[f, 0:8, :] + spec_ref[f, 8:16, :] + spec_ref[f, 16:24, :] + spec_ref[f, 24:32, :]
        acc = acc + WIDTH[f] * s
        acc4 = acc4 + WIDTH[f] * spec_ref[f, 32:36, :]
    energy = jnp.sum(acc, axis=0, keepdims=True) + jnp.sum(acc4, axis=0, keepdims=True)
    load = 0.4 * (energy / (energy + 10.0))
    wd = wd_ref[...]
    cw, sw = jnp.cos(wd), jnp.sin(wd)
    wg = wg_ref[...]
    for d in range(ND):
        lobe = jnp.maximum(COS[d] * cw + SIN[d] * sw, 0.0)
        r_ref[d : d + 1, :] = wg * (lobe * lobe) - load
    r32 = r_ref[0:32, :]
    r4 = r_ref[32:36, :]
    for f in range(0, NF, 2):
        base = 36 * f
        if f == NF - 1:
            v_ref[base : base + 32, :] = spec_ref[f, 0:32, :] * jnp.exp(RATIO[f] * r_ref[0:32, :])
            v_ref[base + 32 : base + 36, :] = spec_ref[f, 32:36, :] * jnp.exp(RATIO[f] * r_ref[32:36, :])
        else:
            g = f + 1
            v_ref[base : base + 32, :] = spec_ref[f, 0:32, :] * jnp.exp(RATIO[f] * r_ref[0:32, :])
            v_ref[base + 32 : base + 64, :] = spec_ref[g, 0:32, :] * jnp.exp(RATIO[g] * r_ref[0:32, :])
            v_ref[base + 64 : base + 68, :] = spec_ref[f, 32:36, :] * jnp.exp(RATIO[f] * r_ref[32:36, :])
            v_ref[base + 68 : base + 72, :] = spec_ref[g, 32:36, :] * jnp.exp(RATIO[g] * r_ref[32:36, :])

    pc = pc_ref[...]
    valid = pc >= 0
    cell = jnp.maximum(pc, 0)
    col_x = cell // (GY * NLAT)
    col_y = cell % (GY * NLAT)
    owner = (col_x // GX) * NLAT + col_y // GY
    local = (col_x % GX) * GY + col_y % GY
    owner = jnp.where(valid, owner, NDEV)
    own = (lax.broadcasted_iota(jnp.int32, (NDEV, CELLS), 0) == owner).astype(F32)
    own16 = own.astype(BF16)
    upper = (
        lax.broadcasted_iota(jnp.int32, (CELLS, CELLS), 0) < lax.broadcasted_iota(jnp.int32, (CELLS, CELLS), 1)
    ).astype(F32).astype(BF16)
    before = nn_dot(own16, upper)
    place = jnp.sum(before * own, axis=0, keepdims=True).astype(jnp.int32)
    target = jnp.where(valid, owner * CAP + place, CELLS)
    oh_ref[...] = (lax.broadcasted_iota(jnp.int32, (CELLS, CELLS), 0) == target).astype(F32).astype(BF16)

    b_ref[...] = jnp.zeros_like(b_ref)
    last = v_ref[128 * NT : 128 * NT + 4, :]
    ident = (local + 1).astype(F32)
    for s in range(CAP):
        here = (place == s).astype(F32)
        b_ref[4 * s : 4 * s + 4, :] = last * here
        b_ref[4 * CAP + s : 4 * CAP + s + 1, :] = ident * here
    bh, bl = split(b_ref[...])
    tail = nt_dot(own16, bh) + nt_dot(own16, bl)
    out_ref[:, 8 * NT, :] = tail

    def group(t, carry):
        hi, lo = split(v_ref[pl.ds(pl.multiple_of(128 * t, 128), 128), :])
        both = nt_dot(oh_ref[...], jnp.concatenate([hi, lo], axis=0))
        res = both[:, :128] + both[:, 128:]
        out_ref[:, pl.ds(pl.multiple_of(8 * t, 8), 8), :] = res.reshape(NDEV, CAP, 128)
        return carry

    lax.fori_loop(0, NT, group, 0)


def source(spectra, wg, wd, pc):
    return pl.pallas_call(
        source_kernel,
        out_shape=jax.ShapeDtypeStruct((NDEV, 64, 128), F32),
        in_specs=[pl.BlockSpec(memory_space=pltpu.VMEM)] * 4,
        out_specs=pl.BlockSpec(memory_space=pltpu.VMEM),
        scratch_shapes=[
            pltpu.VMEM((40, CELLS), F32),
            pltpu.VMEM((904, CELLS), F32),
            pltpu.VMEM((CELLS, CELLS), BF16),
            pltpu.VMEM((128, CELLS), F32),
        ],
        compiler_params=pltpu.CompilerParams(vmem_limit_bytes=VMEM_LIMIT),
        name="source",
    )(spectra, wg.reshape(1, CELLS), wd.reshape(1, CELLS), pc.reshape(1, CELLS))


def exchange_kernel(a_ref, o_ref, send_sem, recv_sem):
    lon = lax.axis_index("lon")
    x = lax.axis_index("lat")
    me = lon * NLAT + x
    c = lon % 2
    z = (lon // 2) % 4
    y = lon // 8

    def partner(r):
        dx = r % 4
        dy = (r // 4 + dx) % 4
        dz = (r // 16 + dx) % 4
        dc = r // 64
        return (((y + dy) % 4) * 4 + (z + dz) % 4) * 2 + (c + dc) % 2, (x + dx) % 4

    barrier = pltpu.get_barrier_semaphore()

    def greet(r, carry):
        pl.semaphore_signal(barrier, 1, device_id=partner(r), device_id_type=MESH)
        return carry

    lax.fori_loop(1, NDEV, greet, 0)
    pl.semaphore_wait(barrier, NDEV - 1)
    rows = pl.ds(0, ROWS)
    pltpu.make_async_copy(a_ref.at[me, rows], o_ref.at[me, rows], recv_sem).start()

    def push(r, carry):
        lo, la = partner(r)
        pltpu.make_async_remote_copy(
            src_ref=a_ref.at[lo * NLAT + la, rows],
            dst_ref=o_ref.at[me, rows],
            send_sem=send_sem,
            recv_sem=recv_sem,
            device_id=(lo, la),
            device_id_type=MESH,
        ).start()
        return carry

    lax.fori_loop(1, NDEV, push, 0)
    pltpu.make_async_copy(o_ref.at[:, rows], o_ref.at[:, rows], recv_sem).wait()
    sent = a_ref.at[pl.ds(0, NDEV - 1), rows]
    pltpu.make_async_copy(sent, sent, send_sem).wait()


def exchange(outgoing):
    return pl.pallas_call(
        exchange_kernel,
        out_shape=jax.ShapeDtypeStruct((NDEV, 64, 128), F32),
        in_specs=[pl.BlockSpec(memory_space=pltpu.VMEM)],
        out_specs=pl.BlockSpec(memory_space=pltpu.VMEM),
        scratch_shapes=[pltpu.SemaphoreType.DMA, pltpu.SemaphoreType.DMA],
        compiler_params=pltpu.CompilerParams(collective_id=0, has_side_effects=True, vmem_limit_bytes=VMEM_LIMIT),
        name="exchange",
    )(outgoing)


def as_tile(ref):
    return jnp.concatenate([ref[i : i + 1, 128 * j : 128 * (j + 1)] for i in range(GX) for j in range(4)], axis=0)


class Lattice:
    def __init__(self):
        sub = lax.broadcasted_iota(jnp.int32, (8, 128), 0)
        lane = lax.broadcasted_iota(jnp.int32, (8, 128), 1)
        self.lane = lane
        self.upper = sub >= 4
        self.lane0 = lane == 0
        self.lane127 = lane == 127
        self.first = (sub % 4 == 0) & self.lane0
        self.last = (sub % 4 == 3) & self.lane127
        self.lane0 = self.lane0 & (sub % 4 != 0)
        self.lane127 = self.lane127 & (sub % 4 != 3)


def lanes(v, k):
    return v if k % 128 == 0 else pltpu.roll(v, k % 128, 1)


def subs(v, k):
    return v if k % 8 == 0 else pltpu.roll(v, k % 8, 0)


def pack(lat, g, up_ref, dn_ref, yp_ref, ym_ref, f):
    for k in range(PHALF):
        up_ref[f, k] = jnp.where(lat.upper, g[CPLUS[k]], subs(g[CPLUS[k + PHALF]], 4))
        dn_ref[f, k] = jnp.where(lat.upper, subs(g[CMINUS[k + PHALF]], 4), g[CMINUS[k]])
    yp = jnp.zeros((8, 128), F32)
    ym = jnp.zeros((8, 128), F32)
    for k in range(18):
        yp = jnp.where(lat.lane == k, lanes(g[SPLUS[k]], k + 1), yp)
        ym = jnp.where(lat.lane == k, lanes(g[SMINUS[k]], k), ym)
    yp_ref[f] = yp
    ym_ref[f] = ym


def substep(lat, field, sh, sea, turns, speed, up, dn, yp, ym):
    yp = subs(yp, 5)
    ym = subs(ym, 3)
    half, pos, neg = [], [], []
    for d in range(ND):
        v = field(d)
        g = sh * v
        if d in CPLUS:
            k = CPLUS.index(d)
            if k < PHALF:
                gx = subs(jnp.where(lat.upper, up(k), g), 4)
            else:
                gx = jnp.where(lat.upper, subs(g, 4), up(k - PHALF))
        else:
            k = CMINUS.index(d)
            if k < PHALF:
                gx = subs(jnp.where(lat.upper, g, dn(k)), 4)
            else:
                gx = jnp.where(lat.upper, dn(k - PHALF), subs(g, 4))
        if d in SPLUS:
            k = SPLUS.index(d)
            r = lanes(g, 1)
            gy = jnp.where(lat.lane0, subs(r, 1), r)
            gy = jnp.where(lat.first, lanes(yp, -k), gy)
        else:
            k = SMINUS.index(d)
            r = lanes(g, 127)
            gy = jnp.where(lat.lane127, subs(r, 7), r)
            gy = jnp.where(lat.last, lanes(ym, 127 - k), gy)
        h = v - (speed * abs(COS[d])) * (g - gx) - (speed * abs(SIN[d])) * (g - gy)
        qt = (speed * turns(d)) * h
        half.append(h)
        pos.append(jnp.maximum(qt, 0.0))
        neg.append(jnp.minimum(qt, 0.0))
    new = []
    for d in range(ND):
        e, w = (d + 1) % ND, (d - 1) % ND
        new.append((half[d] - (pos[d] + neg[e]) + (pos[w] + neg[d])) * sea)
    return new


def fill_turns(turn_ref, sx_ref, sy_ref):
    sx, sy = as_tile(sx_ref), as_tile(sy_ref)
    for d in range(ND):
        turn_ref[d] = SIN[d] * sx - COS[d] * sy


def place_kernel(
    in_ref, mask_ref, sh_ref, sx_ref, sy_ref,
    f1_ref, up_in, dn_in, yp_in, ym_in,
    oh_ref, field_ref, turn_ref, up_out, dn_out, yp_out, ym_out, up2, dn2, yp2, ym2, up1, dn1, yp1, ym1,
    send_sem, recv_sem,
):
    lon = lax.axis_index("lon")
    x = lax.axis_index("lat")
    nxt = (lax.rem(lon + 1, NLON), x)
    prv = (lax.rem(lon + NLON - 1, NLON), x)
    ynxt = (lon, lax.rem(x + 1, NLAT))
    yprv = (lon, lax.rem(x + NLAT - 1, NLAT))
    barrier = pltpu.get_barrier_semaphore()
    for who in (nxt, prv, ynxt, yprv):
        pl.semaphore_signal(barrier, 1, device_id=who, device_id_type=MESH)

    sh = as_tile(sh_ref)
    sea = as_tile(mask_ref).astype(F32)
    fill_turns(turn_ref, sx_ref, sy_ref)
    lat = Lattice()

    tail = in_ref[:, 8 * NT, :]
    ident = tail[:, 4 * CAP : 5 * CAP]
    spread = (
        lax.broadcasted_iota(jnp.int32, (CAP, CELLS), 1) % CAP == lax.broadcasted_iota(jnp.int32, (CAP, CELLS), 0)
    ).astype(F32).astype(BF16)
    ih, il = split(ident)
    wide = nn_dot(ih, spread) + nn_dot(il, spread)
    mine = lax.broadcasted_iota(jnp.int32, (NDEV, CELLS), 1) // CAP == lax.broadcasted_iota(jnp.int32, (NDEV, CELLS), 0)
    ids = jnp.sum(jnp.where(mine, wide, 0.0), axis=0, keepdims=True).astype(jnp.int32) - 1
    oh_ref[...] = (lax.broadcasted_iota(jnp.int32, (CELLS, CELLS), 0) == ids).astype(F32).astype(BF16)

    def unplace(t, carry):
        hi, lo = split(in_ref[:, pl.ds(pl.multiple_of(8 * t, 8), 8), :].reshape(CELLS, 128))
        both = nn_dot(oh_ref[...], jnp.concatenate([hi, lo], axis=1))
        res = both[:, :128] + both[:, 128:]
        for ct in range(8):
            field_ref[pl.ds(pl.multiple_of(128 * t, 128), 128), ct, :] = res[128 * ct : 128 * (ct + 1), :].T
        return carry

    lax.fori_loop(0, NT, unplace, 0)
    cols = []
    for c in range(4):
        pick = (
            lax.broadcasted_iota(jnp.int32, (128, CELLS), 0) == 4 * (lax.broadcasted_iota(jnp.int32, (128, CELLS), 1) % CAP) + c
        ).astype(F32).astype(BF16)
        th, tl = split(tail)
        w = nn_dot(th, pick) + nn_dot(tl, pick)
        cols.append(jnp.sum(jnp.where(mine, w, 0.0), axis=0, keepdims=True))
    ch, cl = split(jnp.concatenate(cols + [jnp.zeros((4, CELLS), F32)], axis=0))
    tailv = nt_dot(ch, oh_ref[...]) + nt_dot(cl, oh_ref[...])
    for ct in range(8):
        field_ref[128 * NT : 128 * NT + 8, ct, :] = tailv[:, 128 * ct : 128 * (ct + 1)]

    def pack_one(f, row):
        g = [sh * field_ref[row(d)] for d in range(ND)]
        pack(lat, g, up_out, dn_out, yp_out, ym_out, f)

    def pack_pair(q, carry):
        base = 72 * q
        pack_one(2 * q, lambda d: base + row_of(0, d))
        pack_one(2 * q + 1, lambda d: base + row_of(1, d))
        return carry

    lax.fori_loop(0, NF // 2, pack_pair, 0)
    pack_one(NF - 1, lambda d: row_of(NF - 1, d))
    pl.semaphore_wait(barrier, 4)

    def copies(outs, ins, which):
        res = []
        for n, (src, dst, who) in enumerate(zip(outs, ins, (nxt, prv, ynxt, yprv))):
            res.append(
                pltpu.make_async_remote_copy(
                    src_ref=src, dst_ref=dst, send_sem=send_sem.at[which, n], recv_sem=recv_sem.at[which, n],
                    device_id=who, device_id_type=MESH,
                )
            )
        return res

    first = copies((up_out, dn_out, yp_out, ym_out), (up1, dn1, yp1, ym1), 0)
    for cp in first:
        cp.start()
    for cp in first:
        cp.wait()

    low = (x > 0).astype(F32)
    high = (x < NLAT - 1).astype(F32)

    def one(f, speed, row):
        new = substep(
            lat, lambda d: field_ref[row(d)], sh, sea, lambda d: turn_ref[d], speed,
            lambda k: up1[f, k], lambda k: dn1[f, k], yp1[f] * low, ym1[f] * high,
        )
        for d in range(ND):
            f1_ref[f, d] = new[d]
        pack(lat, [sh * v for v in new], up2, dn2, yp2, ym2, f)

    def pair(q, speed):
        base = 72 * q
        one(2 * q, speed, lambda d: base + row_of(0, d))
        one(2 * q + 1, speed * (1.0 / 1.1), lambda d: base + row_of(1, d))
        return speed * (1.0 / 1.21)

    speed = lax.fori_loop(0, NF // 2, pair, jnp.float32(0.65))
    one(NF - 1, speed, lambda d: row_of(NF - 1, d))
    second = copies((up2, dn2, yp2, ym2), (up_in, dn_in, yp_in, ym_in), 1)
    for cp in second:
        cp.start()
    for cp in second:
        cp.wait()


def face_shapes():
    return [(NF, PHALF, 8, 128), (NF, PHALF, 8, 128), (NF, 8, 128), (NF, 8, 128)]


def place(incoming, mask, sh, sx, sy):
    faces = [pltpu.VMEM(s, F32) for s in face_shapes()]
    return pl.pallas_call(
        place_kernel,
        out_shape=[jax.ShapeDtypeStruct((NF, ND, 8, 128), F32)] + [jax.ShapeDtypeStruct(s, F32) for s in face_shapes()],
        in_specs=[pl.BlockSpec(memory_space=pltpu.VMEM)] * 5,
        out_specs=[pl.BlockSpec(memory_space=pltpu.VMEM)] * 5,
        scratch_shapes=[
            pltpu.VMEM((CELLS, CELLS), BF16),
            pltpu.VMEM((904, 8, 128), F32),
            pltpu.VMEM((ND, 8, 128), F32),
        ]
        + faces * 3
        + [pltpu.SemaphoreType.DMA((2, 4)), pltpu.SemaphoreType.DMA((2, 4))],
        compiler_params=pltpu.CompilerParams(collective_id=1, has_side_effects=True, vmem_limit_bytes=VMEM_LIMIT),
        name="place",
    )(incoming, mask, sh, sx, sy)


def finish_kernel(f1_ref, up_ref, dn_ref, yp_ref, ym_ref, edge_ref, mask_ref, sh_ref, sx_ref, sy_ref, out_ref, turn_ref):
    sh = as_tile(sh_ref)
    sea = as_tile(mask_ref).astype(F32)
    fill_turns(turn_ref, sx_ref, sy_ref)
    lat = Lattice()
    x = edge_ref[0]
    low = (x > 0).astype(F32)
    high = (x < NLAT - 1).astype(F32)

    def one(f, speed):
        new = substep(
            lat, lambda d: f1_ref[f, d], sh, sea, lambda d: turn_ref[d], speed,
            lambda k: up_ref[f, k], lambda k: dn_ref[f, k], yp_ref[f] * low, ym_ref[f] * high,
        )
        for d in range(ND):
            out_ref[f, d, pl.ds(0, 4, 2), :] = new[d][0:4, :]
            out_ref[f, d, pl.ds(1, 4, 2), :] = new[d][4:8, :]
        return speed * (1.0 / 1.1)

    lax.fori_loop(0, NF, one, jnp.float32(0.65))


def finish(f1, up, dn, yp, ym, mask, sh, sx, sy):
    edge = lax.axis_index("lat").astype(jnp.int32).reshape(1)
    return pl.pallas_call(
        finish_kernel,
        out_shape=jax.ShapeDtypeStruct((NF, ND, 8, 128), F32),
        in_specs=[pl.BlockSpec(memory_space=pltpu.VMEM)] * 5
        + [pl.BlockSpec(memory_space=pltpu.SMEM)]
        + [pl.BlockSpec(memory_space=pltpu.VMEM)] * 4,
        out_specs=pl.BlockSpec(memory_space=pltpu.VMEM),
        scratch_shapes=[pltpu.VMEM((ND, 8, 128), F32)],
        compiler_params=pltpu.CompilerParams(vmem_limit_bytes=VMEM_LIMIT),
        name="finish",
    )(f1, up, dn, yp, ym, edge, mask, sh, sx, sy)


def on_device(spectra, wind_growth, wind_dir, point_cell, land_mask, shoaling, slope_x, slope_y):
    outgoing = source(spectra, wind_growth, wind_dir, point_cell)
    incoming = exchange(outgoing)
    f1, up, dn, yp, ym = place(incoming, land_mask, shoaling, slope_x, slope_y)
    out = finish(f1, up, dn, yp, ym, land_mask, shoaling, slope_x, slope_y)
    out = out.reshape(NF, ND, 4, GX, 128)
    return jnp.transpose(out, (0, 1, 3, 2, 4)).reshape(NF, ND, GX, GY)


def solution(mesh):
    placed = (
        P(None, None, ("lon", "lat")),
        P(("lon", "lat")),
        P(("lon", "lat")),
        P(("lon", "lat")),
        P("lon", "lat"),
        P("lon", "lat"),
        P("lon", "lat"),
        P("lon", "lat"),
    )
    return jax.shard_map(
        on_device, mesh=mesh, in_specs=placed, out_specs=P(None, None, "lon", "lat"), check_vma=False
    )
```

```python
import math

import jax
import jax.numpy as jnp
from jax import lax
from jax.experimental import pallas as pl
from jax.experimental.pallas import tpu as pltpu
from jax.sharding import PartitionSpec as P

MESH = pl.DeviceIdType.MESH
F32 = jnp.float32
BF16 = jnp.bfloat16

NF, ND = 25, 36
GX, GY = 2, 512
NLON, NLAT = 32, 4
NDEV = NLON * NLAT
CELLS = GX * GY
CAP = CELLS // NDEV
NT = 7
ROWS = 57
DTH = 2.0 * math.pi / ND
THETA = [(d + 0.5) * DTH for d in range(ND)]
COS = [math.cos(t) for t in THETA]
SIN = [math.sin(t) for t in THETA]
RATIO = [1.1 ** (f - (NF - 1)) for f in range(NF)]
WIDTH = [0.1 * 1.1**f * DTH for f in range(NF)]
CPLUS = [d for d in range(27, 36)] + [d for d in range(0, 9)]
CMINUS = [d for d in range(9, 27)]
SPLUS = list(range(0, 18))
SMINUS = list(range(18, 36))
PHALF = 9
VMEM_LIMIT = 60 << 20


def row_of(f, d):
    if f == NF - 1:
        return 36 * (NF - 1) + d
    base = 72 * (f // 2)
    if d < 32:
        return base + 32 * (f % 2) + d
    return base + 64 + 4 * (f % 2) + (d - 32)


def row_dyn(f, d):
    base = 72 * lax.div(f, 2)
    if d < 32:
        return base + 32 * lax.rem(f, 2) + d
    return base + jnp.where(f == NF - 1, 32, 64 + 4 * lax.rem(f, 2)) + (d - 32)


def whole(t):
    t = jnp.clip(t, 0, NT)
    return 2 * lax.div(16 * t, 9) + lax.div(t, NT)


def split(v):
    hi = v.astype(BF16)
    lo = (v - hi.astype(F32)).astype(BF16)
    return hi, lo


def nt_dot(a, b):
    return lax.dot_general(a, b, (((1,), (1,)), ((), ())), preferred_element_type=F32)


def nn_dot(a, b):
    return lax.dot_general(a, b, (((1,), (0,)), ((), ())), preferred_element_type=F32)


def as_tile(ref):
    return jnp.concatenate([ref[i : i + 1, 128 * j : 128 * (j + 1)] for i in range(GX) for j in range(4)], axis=0)


class Lattice:
    def __init__(self):
        sub = lax.broadcasted_iota(jnp.int32, (8, 128), 0)
        lane = lax.broadcasted_iota(jnp.int32, (8, 128), 1)
        self.lane = lane
        self.upper = sub >= 4
        self.lane0 = lane == 0
        self.lane127 = lane == 127
        self.first = (sub % 4 == 0) & self.lane0
        self.last = (sub % 4 == 3) & self.lane127
        self.lane0 = self.lane0 & (sub % 4 != 0)
        self.lane127 = self.lane127 & (sub % 4 != 3)


def lanes(v, k):
    return v if k % 128 == 0 else pltpu.roll(v, k % 128, 1)


def subs(v, k):
    return v if k % 8 == 0 else pltpu.roll(v, k % 8, 0)


def pack(lat, g, up_ref, dn_ref, yp_ref, ym_ref):
    for k in range(PHALF):
        up_ref[k] = jnp.where(lat.upper, g[CPLUS[k]], subs(g[CPLUS[k + PHALF]], 4))
        dn_ref[k] = jnp.where(lat.upper, subs(g[CMINUS[k + PHALF]], 4), g[CMINUS[k]])
    yp = jnp.zeros((8, 128), F32)
    ym = jnp.zeros((8, 128), F32)
    for k in range(18):
        yp = jnp.where(lat.lane == k, lanes(g[SPLUS[k]], k + 1), yp)
        ym = jnp.where(lat.lane == k, lanes(g[SMINUS[k]], k), ym)
    yp_ref[...] = yp
    ym_ref[...] = ym


def substep(lat, field, sh, sea, turns, speed, up, dn, yp, ym):
    yp = subs(yp, 5)
    ym = subs(ym, 3)
    half, pos, neg = [], [], []
    for d in range(ND):
        v = field(d)
        g = sh * v
        if d in CPLUS:
            k = CPLUS.index(d)
            if k < PHALF:
                gx = subs(jnp.where(lat.upper, up(k), g), 4)
            else:
                gx = jnp.where(lat.upper, subs(g, 4), up(k - PHALF))
        else:
            k = CMINUS.index(d)
            if k < PHALF:
                gx = subs(jnp.where(lat.upper, g, dn(k)), 4)
            else:
                gx = jnp.where(lat.upper, dn(k - PHALF), subs(g, 4))
        if d in SPLUS:
            k = SPLUS.index(d)
            r = lanes(g, 1)
            gy = jnp.where(lat.lane0, subs(r, 1), r)
            gy = jnp.where(lat.first, lanes(yp, -k), gy)
        else:
            k = SMINUS.index(d)
            r = lanes(g, 127)
            gy = jnp.where(lat.lane127, subs(r, 7), r)
            gy = jnp.where(lat.last, lanes(ym, 127 - k), gy)
        h = v - (speed * abs(COS[d])) * (g - gx) - (speed * abs(SIN[d])) * (g - gy)
        qt = (speed * turns(d)) * h
        half.append(h)
        pos.append(jnp.maximum(qt, 0.0))
        neg.append(jnp.minimum(qt, 0.0))
    new = []
    for d in range(ND):
        e, w = (d + 1) % ND, (d - 1) % ND
        new.append((half[d] - (pos[d] + neg[e]) + (pos[w] + neg[d])) * sea)
    return new


def fill_turns(turn_ref, sx_ref, sy_ref):
    sx, sy = as_tile(sx_ref), as_tile(sy_ref)
    for d in range(ND):
        turn_ref[d] = SIN[d] * sx - COS[d] * sy


def step_kernel(
    spec_hbm, wg_ref, wd_ref, pc_ref, mask_ref, sh_ref, sx_ref, sy_ref, out_hbm,
    spec_ref, r_ref, v_ref, b_ref, sbuf, rbuf, ohs_ref, ohr_ref, field_ref, f1_ref, stage_ref, turn_ref,
    up_out, dn_out, yp_out, ym_out, up_in, dn_in, yp_in, ym_in, table,
    spec_sem, send_sem, recv_sem, face_send, face_recv, out_sem,
):
    lon = lax.axis_index("lon")
    x = lax.axis_index("lat")
    me = lon * NLAT + x
    c = lax.rem(lon, 2)
    z = lax.rem(lax.div(lon, 2), 4)
    y = lax.div(lon, 8)
    nxt = (lax.rem(lon + 1, NLON), x)
    prv = (lax.rem(lon + NLON - 1, NLON), x)
    ynxt = (lon, lax.rem(x + 1, NLAT))
    yprv = (lon, lax.rem(x + NLAT - 1, NLAT))

    loads = [
        pltpu.make_async_copy(spec_hbm.at[pl.ds(5 * i, 5)], spec_ref.at[pl.ds(5 * i, 5)], spec_sem.at[i])
        for i in range(5)
    ]
    for cp in loads:
        cp.start()

    barrier = pltpu.get_barrier_semaphore()

    def greet(r, carry):
        who = lax.rem(me + r, NDEV)
        pl.semaphore_signal(barrier, 1, device_id=(lax.div(who, NLAT), lax.rem(who, NLAT)), device_id_type=MESH)
        return carry

    lax.fori_loop(1, NDEV, greet, 0)
    for f in range(NF):
        table[f] = jnp.float32(RATIO[f])
        table[32 + f] = jnp.float32(0.65 * 1.1 ** (-f))

    pc = pc_ref[...]
    valid = pc >= 0
    cell = jnp.maximum(pc, 0)
    col_x = cell // (GY * NLAT)
    col_y = cell % (GY * NLAT)
    owner = (col_x // GX) * NLAT + col_y // GY
    local = (col_x % GX) * GY + col_y % GY
    owner = jnp.where(valid, owner, NDEV)
    own = (lax.broadcasted_iota(jnp.int32, (NDEV, CELLS), 0) == owner).astype(F32)
    own16 = own.astype(BF16)
    ohs_ref[...] = (
        lax.broadcasted_iota(jnp.int32, (CELLS, CELLS), 0) < lax.broadcasted_iota(jnp.int32, (CELLS, CELLS), 1)
    ).astype(F32).astype(BF16)
    before = nn_dot(own16, ohs_ref[...])
    where = jnp.sum(before * own, axis=0, keepdims=True).astype(jnp.int32)
    target = jnp.where(valid, owner * CAP + where, CELLS)
    ohs_ref[...] = (lax.broadcasted_iota(jnp.int32, (CELLS, CELLS), 0) == target).astype(F32).astype(BF16)

    wd = wd_ref[...]
    cw, sw = jnp.cos(wd), jnp.sin(wd)
    wg = wg_ref[...]
    acc = jnp.zeros((8, CELLS), F32)
    acc4 = jnp.zeros((4, CELLS), F32)
    for f in range(NF):
        if f % 5 == 0:
            loads[f // 5].wait()
        s = spec_ref[f, 0:8, :] + spec_ref[f, 8:16, :] + spec_ref[f, 16:24, :] + spec_ref[f, 24:32, :]
        acc = acc + WIDTH[f] * s
        acc4 = acc4 + WIDTH[f] * spec_ref[f, 32:36, :]
    energy = jnp.sum(acc, axis=0, keepdims=True) + jnp.sum(acc4, axis=0, keepdims=True)
    load = 0.4 * (energy / (energy + 10.0))
    for d in range(ND):
        lobe = jnp.maximum(COS[d] * cw + SIN[d] * sw, 0.0)
        r_ref[d : d + 1, :] = wg * (lobe * lobe) - load

    last_base = 36 * (NF - 1)
    v_ref[last_base : last_base + 32, :] = spec_ref[NF - 1, 0:32, :] * jnp.exp(RATIO[NF - 1] * r_ref[0:32, :])
    v_ref[last_base + 32 : last_base + 36, :] = spec_ref[NF - 1, 32:36, :] * jnp.exp(RATIO[NF - 1] * r_ref[32:36, :])

    b_ref[...] = jnp.zeros_like(b_ref)
    last = v_ref[128 * NT : 128 * NT + 4, :]
    ident = (local + 1).astype(F32)
    for s in range(CAP):
        here = (where == s).astype(F32)
        b_ref[4 * s : 4 * s + 4, :] = last * here
        b_ref[4 * CAP + s : 4 * CAP + s + 1, :] = ident * here
    bh, bl = split(b_ref[...])
    sbuf[:, 8 * NT, :] = nt_dot(own16, bh) + nt_dot(own16, bl)

    def push(rows, sem):
        pltpu.make_async_copy(sbuf.at[me, rows], rbuf.at[me, rows], sem).start()

        def go(j, carry):
            b, e, dc = lax.rem(j, 4), lax.rem(lax.div(j, 4), 4), lax.div(j, 16)
            cc = lax.rem(c + dc, 2)
            for a in range(4):
                lo = (lax.rem(y + b + a, 4) * 4 + lax.rem(z + e + a, 4)) * 2 + cc
                la = lax.rem(x + a, 4)
                copy = pltpu.make_async_remote_copy(
                    src_ref=sbuf.at[lo * NLAT + la, rows], dst_ref=rbuf.at[me, rows],
                    send_sem=send_sem, recv_sem=sem, device_id=(lo, la), device_id_type=MESH,
                )
                if a == 0:
                    pl.when(j > 0)(copy.start)
                else:
                    copy.start()
            return carry

        lax.fori_loop(0, NDEV // 4, go, 0)

    def tile(t):
        return pl.ds(pl.multiple_of(8 * t, 8), 8)

    def arrive(rows, sem):
        pltpu.make_async_copy(rbuf.at[:, rows], rbuf.at[:, rows], sem).wait()

    def grow(q, carry):
        base = pl.multiple_of(72 * q, 8)
        f, g = 2 * q, 2 * q + 1
        e4 = []
        for i, h in enumerate((f, g)):
            ratio = table[h]
            v_ref[pl.ds(base + 32 * i, 32), :] = spec_ref[h, 0:32, :] * jnp.exp(ratio * r_ref[0:32, :])
            e4.append(spec_ref[h, 32:36, :] * jnp.exp(ratio * r_ref[32:36, :]))
        v_ref[pl.ds(base + 64, 8), :] = jnp.concatenate(e4, axis=0)
        return carry

    def pairs(t):
        return jnp.where(t == 0, 0, jnp.minimum(lax.div(16 * t + 8, 9), NF // 2))

    def group(t):
        lax.fori_loop(pairs(t), pairs(t + 1), grow, 0)
        hi, lo = split(v_ref[pl.ds(pl.multiple_of(128 * t, 128), 128), :])
        both = nt_dot(ohs_ref[...], jnp.concatenate([hi, lo], axis=0))
        res = both[:, :128] + both[:, 128:]
        sbuf[:, tile(t), :] = res.reshape(NDEV, CAP, 128)

    pl.semaphore_wait(barrier, NDEV - 1)
    push(pl.ds(8 * NT, 1), recv_sem.at[NT])

    def prologue(t, carry):
        group(t)

        @pl.when(t < 2)
        def _():
            push(tile(t), recv_sem.at[t])

        return carry

    lax.fori_loop(0, 3, prologue, 0)

    sh = as_tile(sh_ref)
    sea = as_tile(mask_ref).astype(F32)
    fill_turns(turn_ref, sx_ref, sy_ref)
    lat = Lattice()
    low = (x > 0).astype(F32)
    high = (x < NLAT - 1).astype(F32)

    arrive(pl.ds(8 * NT, 1), recv_sem.at[NT])
    tail = rbuf[:, 8 * NT, :]
    ident = tail[:, 4 * CAP : 5 * CAP]
    spread = (
        lax.broadcasted_iota(jnp.int32, (CAP, CELLS), 1) % CAP == lax.broadcasted_iota(jnp.int32, (CAP, CELLS), 0)
    ).astype(F32).astype(BF16)
    ih, il = split(ident)
    wide = nn_dot(ih, spread) + nn_dot(il, spread)
    mine = lax.broadcasted_iota(jnp.int32, (NDEV, CELLS), 1) // CAP == lax.broadcasted_iota(jnp.int32, (NDEV, CELLS), 0)
    ids = jnp.sum(jnp.where(mine, wide, 0.0), axis=0, keepdims=True).astype(jnp.int32) - 1
    ohr_ref[...] = (lax.broadcasted_iota(jnp.int32, (CELLS, CELLS), 0) == ids).astype(F32).astype(BF16)
    cols = []
    th, tl = split(tail)
    for k in range(4):
        pick = (
            lax.broadcasted_iota(jnp.int32, (128, CELLS), 0) == 4 * (lax.broadcasted_iota(jnp.int32, (128, CELLS), 1) % CAP) + k
        ).astype(F32).astype(BF16)
        w = nn_dot(th, pick) + nn_dot(tl, pick)
        cols.append(jnp.sum(jnp.where(mine, w, 0.0), axis=0, keepdims=True))
    ch, cl = split(jnp.concatenate(cols + [jnp.zeros((4, CELLS), F32)], axis=0))
    tailv = nt_dot(ch, ohr_ref[...]) + nt_dot(cl, ohr_ref[...])
    for ct in range(8):
        field_ref[128 * NT : 128 * NT + 8, ct, :] = tailv[:, 128 * ct : 128 * (ct + 1)]

    def unplace(t):
        hi, lo = split(rbuf[:, tile(t), :].reshape(CELLS, 128))
        both = nn_dot(ohr_ref[...], jnp.concatenate([hi, lo], axis=1))
        res = both[:, :128] + both[:, 128:]
        for ct in range(8):
            field_ref[pl.ds(pl.multiple_of(128 * t, 128), 128), ct, :] = res[128 * ct : 128 * (ct + 1), :].T

    def faces(s, f):
        bufs = zip((up_out, dn_out, yp_out, ym_out), (up_in, dn_in, yp_in, ym_in), (nxt, prv, ynxt, yprv))
        return [
            pltpu.make_async_remote_copy(
                src_ref=src.at[s, f], dst_ref=dst.at[s, f], send_sem=face_send.at[s, n],
                recv_sem=face_recv.at[s, n, f], device_id=who, device_id_type=MESH,
            )
            for n, (src, dst, who) in enumerate(bufs)
        ]

    def send(s, f):
        for copy in faces(s, f):
            copy.start()

    def await_faces(s, f):
        for copy in faces(s, f):
            copy.wait_recv()

    def wrap(s, f, g):
        pack(lat, g, up_out.at[s, f], dn_out.at[s, f], yp_out.at[s, f], ym_out.at[s, f])

    def propagate(s, f, get):
        await_faces(s, f)
        return substep(
            lat, get, sh, sea, lambda d: turn_ref[d], table[32 + f],
            lambda k: up_in[s, f, k], lambda k: dn_in[s, f, k], yp_in[s, f] * low, ym_in[s, f] * high,
        )

    def over(lo, hi, fn):
        def body(f, carry):
            fn(f)
            return carry

        lax.fori_loop(lo, hi, body, 0)

    def start_face(f):
        wrap(0, f, [sh * field_ref[row_dyn(f, d)] for d in range(ND)])

    def first(f):
        new = propagate(0, f, lambda d: field_ref[row_dyn(f, d)])
        for d in range(ND):
            f1_ref[f, d] = new[d]
        wrap(1, f, [sh * v for v in new])

    def second(f):
        new = propagate(1, f, lambda d: f1_ref[f, d])
        for d in range(ND):
            stage_ref[f, d, pl.ds(0, 4, 2), :] = new[d][0:4, :]
            stage_ref[f, d, pl.ds(1, 4, 2), :] = new[d][4:8, :]

    def emit(f):
        pltpu.make_async_copy(stage_ref.at[f], out_hbm.at[f], out_sem).start()

    def step(t, carry):
        @pl.when(t < NT)
        def _():
            arrive(tile(t), recv_sem.at[t])
            unplace(t)

        over(whole(t), whole(t + 1), start_face)
        over(whole(t), whole(t + 1), lambda f: send(0, f))

        @pl.when(t + 2 < NT)
        def _():
            push(tile(t + 2), recv_sem.at[t + 2])

        @pl.when(t + 3 < NT)
        def _():
            group(t + 3)

        over(whole(t - 1), whole(t), first)
        over(whole(t - 1), whole(t), lambda f: send(1, f))
        over(whole(t - 2), whole(t - 1), second)
        over(whole(t - 2), whole(t - 1), emit)
        return carry

    lax.fori_loop(0, NT + 2, step, 0)
    sent = sbuf.at[pl.ds(0, NDEV - 1), pl.ds(0, ROWS)]
    pltpu.make_async_copy(sent, sent, send_sem).wait()
    for s in range(2):
        for n, src in enumerate((up_out, dn_out, yp_out, ym_out)):
            pltpu.make_async_copy(src.at[s], src.at[s], face_send.at[s, n]).wait()
    pltpu.make_async_copy(stage_ref, out_hbm, out_sem).wait()


def on_device(spectra, wind_growth, wind_dir, point_cell, land_mask, shoaling, slope_x, slope_y):
    face = [(2, NF, PHALF, 8, 128), (2, NF, PHALF, 8, 128), (2, NF, 8, 128), (2, NF, 8, 128)]
    out = pl.pallas_call(
        step_kernel,
        out_shape=jax.ShapeDtypeStruct((NF, ND, 8, 128), F32),
        in_specs=[pl.BlockSpec(memory_space=pl.ANY)] + [pl.BlockSpec(memory_space=pltpu.VMEM)] * 7,
        out_specs=pl.BlockSpec(memory_space=pl.ANY),
        scratch_shapes=[
            pltpu.VMEM((NF, ND, CELLS), F32),
            pltpu.VMEM((40, CELLS), F32),
            pltpu.VMEM((904, CELLS), F32),
            pltpu.VMEM((128, CELLS), F32),
            pltpu.VMEM((NDEV, 64, 128), F32),
            pltpu.VMEM((NDEV, 64, 128), F32),
            pltpu.VMEM((CELLS, CELLS), BF16),
            pltpu.VMEM((CELLS, CELLS), BF16),
            pltpu.VMEM((904, 8, 128), F32),
            pltpu.VMEM((NF, ND, 8, 128), F32),
            pltpu.VMEM((NF, ND, 8, 128), F32),
            pltpu.VMEM((ND, 8, 128), F32),
        ]
        + [pltpu.VMEM(s, F32) for s in face] * 2
        + [
            pltpu.SMEM((64,), F32),
            pltpu.SemaphoreType.DMA((5,)),
            pltpu.SemaphoreType.DMA,
            pltpu.SemaphoreType.DMA((NT + 1,)),
            pltpu.SemaphoreType.DMA((2, 4)),
            pltpu.SemaphoreType.DMA((2, 4, NF)),
            pltpu.SemaphoreType.DMA,
        ],
        compiler_params=pltpu.CompilerParams(collective_id=0, has_side_effects=True, vmem_limit_bytes=VMEM_LIMIT),
        name="wave_step",
    )(
        spectra, wind_growth.reshape(1, CELLS), wind_dir.reshape(1, CELLS), point_cell.reshape(1, CELLS),
        land_mask, shoaling, slope_x, slope_y,
    )
    out = out.reshape(NF, ND, 4, GX, 128)
    return jnp.transpose(out, (0, 1, 3, 2, 4)).reshape(NF, ND, GX, GY)


def solution(mesh):
    placed = (
        P(None, None, ("lon", "lat")),
        P(("lon", "lat")),
        P(("lon", "lat")),
        P(("lon", "lat")),
        P("lon", "lat"),
        P("lon", "lat"),
        P("lon", "lat"),
        P("lon", "lat"),
    )
    return jax.shard_map(
        on_device, mesh=mesh, in_specs=placed, out_specs=P(None, None, "lon", "lat"), check_vma=False
    )
```

```python
import functools
import math

import jax
import jax.numpy as jnp
from jax import lax
from jax.experimental import pallas as pl
from jax.experimental.pallas import tpu as pltpu
from jax.sharding import PartitionSpec as P

MESH = pl.DeviceIdType.MESH
F32 = jnp.float32
BF16 = jnp.bfloat16

NF, ND = 25, 36
GX, GY = 2, 512
NLON, NLAT = 32, 4
NDEV = NLON * NLAT
CELLS = GX * GY
CAP = CELLS // NDEV
NT = 7
ROWS = 57
DTH = 2.0 * math.pi / ND
THETA = [(d + 0.5) * DTH for d in range(ND)]
COS = [math.cos(t) for t in THETA]
SIN = [math.sin(t) for t in THETA]
RATIO = [1.1 ** (f - (NF - 1)) for f in range(NF)]
WIDTH = [0.1 * 1.1**f * DTH for f in range(NF)]
CPLUS = [d for d in range(27, 36)] + [d for d in range(0, 9)]
CMINUS = [d for d in range(9, 27)]
SPLUS = list(range(0, 18))
SMINUS = list(range(18, 36))
PHALF = 9
VMEM_LIMIT = 60 << 20


def row_of(f, d):
    if f == NF - 1:
        return 36 * (NF - 1) + d
    base = 72 * (f // 2)
    if d < 32:
        return base + 32 * (f % 2) + d
    return base + 64 + 4 * (f % 2) + (d - 32)


def row_dyn(f, d):
    base = 72 * lax.div(f, 2)
    if d < 32:
        return base + 32 * lax.rem(f, 2) + d
    return base + jnp.where(f == NF - 1, 32, 64 + 4 * lax.rem(f, 2)) + (d - 32)


def whole(t):
    t = jnp.clip(t, 0, NT)
    return 2 * lax.div(16 * t, 9) + lax.div(t, NT)


def split(v):
    hi = v.astype(BF16)
    lo = (v - hi.astype(F32)).astype(BF16)
    return hi, lo


def nt_dot(a, b):
    return lax.dot_general(a, b, (((1,), (1,)), ((), ())), preferred_element_type=F32)


def nn_dot(a, b):
    return lax.dot_general(a, b, (((1,), (0,)), ((), ())), preferred_element_type=F32)


def as_tile(ref):
    return jnp.concatenate([ref[i : i + 1, 128 * j : 128 * (j + 1)] for i in range(GX) for j in range(4)], axis=0)


class Lattice:
    def __init__(self):
        sub = lax.broadcasted_iota(jnp.int32, (8, 128), 0)
        lane = lax.broadcasted_iota(jnp.int32, (8, 128), 1)
        self.lane = lane
        self.upper = sub >= 4
        self.lane0 = lane == 0
        self.lane127 = lane == 127
        self.first = (sub % 4 == 0) & self.lane0
        self.last = (sub % 4 == 3) & self.lane127
        self.lane0 = self.lane0 & (sub % 4 != 0)
        self.lane127 = self.lane127 & (sub % 4 != 3)


def lanes(v, k):
    return v if k % 128 == 0 else pltpu.roll(v, k % 128, 1)


def subs(v, k):
    return v if k % 8 == 0 else pltpu.roll(v, k % 8, 0)


class Faces:
    def __init__(self, lat, up_ref, dn_ref, yp_ref, ym_ref):
        self.lat, self.up, self.dn, self.yp_ref, self.ym_ref = lat, up_ref, dn_ref, yp_ref, ym_ref
        self.yp = jnp.zeros((8, 128), F32)
        self.ym = jnp.zeros((8, 128), F32)

    def put(self, d, g):
        if d in CPLUS:
            k = CPLUS.index(d)
            if k < PHALF:
                self.up[k, 4:8, :] = g[4:8, :]
            else:
                self.up[k - PHALF, 0:4, :] = g[4:8, :]
        else:
            k = CMINUS.index(d)
            if k < PHALF:
                self.dn[k, 0:4, :] = g[0:4, :]
            else:
                self.dn[k - PHALF, 4:8, :] = g[0:4, :]
        if d in SPLUS:
            k = SPLUS.index(d)
            self.yp = jnp.where(self.lat.lane == k, lanes(g, k + 1), self.yp)
        else:
            k = SMINUS.index(d)
            self.ym = jnp.where(self.lat.lane == k, lanes(g, k), self.ym)

    def close(self):
        self.yp_ref[...] = self.yp
        self.ym_ref[...] = self.ym


def substep(lat, field, sh, sea, turns, speed, up, dn, yp, ym, put):
    yp = subs(yp, 5)
    ym = subs(ym, 3)

    def moved(d):
        v = field(d)
        g = sh * v
        if d in CPLUS:
            k = CPLUS.index(d)
            if k < PHALF:
                gx = subs(jnp.where(lat.upper, up(k), g), 4)
            else:
                gx = jnp.where(lat.upper, subs(g, 4), up(k - PHALF))
        else:
            k = CMINUS.index(d)
            if k < PHALF:
                gx = subs(jnp.where(lat.upper, g, dn(k)), 4)
            else:
                gx = jnp.where(lat.upper, dn(k - PHALF), subs(g, 4))
        if d in SPLUS:
            k = SPLUS.index(d)
            r = lanes(g, 1)
            gy = jnp.where(lat.lane0, subs(r, 1), r)
            gy = jnp.where(lat.first, lanes(yp, -k), gy)
        else:
            k = SMINUS.index(d)
            r = lanes(g, 127)
            gy = jnp.where(lat.lane127, subs(r, 7), r)
            gy = jnp.where(lat.last, lanes(ym, 127 - k), gy)
        h = v - (speed * abs(COS[d])) * (g - gx) - (speed * abs(SIN[d])) * (g - gy)
        qt = (speed * turns(d)) * h
        return h, jnp.maximum(qt, 0.0), jnp.minimum(qt, 0.0)

    begin = moved(0)
    end = moved(ND - 1)
    west, here = end, begin
    for d in range(ND):
        east = begin if d == ND - 1 else (end if d == ND - 2 else moved(d + 1))
        put(d, (here[0] - (here[1] + east[2]) + (west[1] + here[2])) * sea)
        west, here = here, east


def fill_turns(turn_ref, sx_ref, sy_ref):
    sx, sy = as_tile(sx_ref), as_tile(sy_ref)
    for d in range(ND):
        turn_ref[d] = SIN[d] * sx - COS[d] * sy


def step_kernel(
    spec_hbm, wg_hbm, wd_hbm, pc_hbm, mask_hbm, sh_hbm, sx_hbm, sy_hbm, out_hbm,
    wg_ref, wd_ref, pc_ref, mask_ref, sh_ref, sx_ref, sy_ref,
    spec_ref, r_ref, v_ref, b_ref, sbuf, rbuf, ohs_ref, ohr_ref, field_ref, f1_ref, stage_ref, turn_ref,
    up_out, dn_out, yp_out, ym_out, up_in, dn_in, yp_in, ym_in, table,
    small_sem, spec_sem, send_sem, recv_sem, face_send, face_recv, out_sem,
):
    lon = lax.axis_index("lon")
    x = lax.axis_index("lat")
    me = lon * NLAT + x
    c = lax.rem(lon, 2)
    z = lax.rem(lax.div(lon, 2), 4)
    y = lax.div(lon, 8)
    nxt = (lax.rem(lon + 1, NLON), x)
    prv = (lax.rem(lon + NLON - 1, NLON), x)
    ynxt = (lon, lax.rem(x + 1, NLAT))
    yprv = (lon, lax.rem(x + NLAT - 1, NLAT))

    barrier = pltpu.get_barrier_semaphore()
    columns = [lax.rem(x + a, NLAT) for a in range(NLAT)]

    def greet(k, carry):
        row = lax.rem(lon + k, NLON)
        for a in range(NLAT):
            signal = functools.partial(
                pl.semaphore_signal, barrier, 1, device_id=(row, columns[a]), device_id_type=MESH
            )
            if a == 0:
                pl.when(k > 0)(signal)
            else:
                signal()
        return carry

    smalls = [
        pltpu.make_async_copy(src, dst, small_sem.at[n])
        for n, (src, dst) in enumerate(
            (
                (pc_hbm, pc_ref), (wd_hbm, wd_ref), (wg_hbm, wg_ref), (mask_hbm, mask_ref),
                (sh_hbm, sh_ref), (sx_hbm, sx_ref), (sy_hbm, sy_ref),
            )
        )
    ]
    for cp in smalls:
        cp.start()
    loads = [
        pltpu.make_async_copy(spec_hbm.at[pl.ds(5 * i, 5)], spec_ref.at[pl.ds(5 * i, 5)], spec_sem.at[i])
        for i in range(5)
    ]
    for cp in loads:
        cp.start()
    lax.fori_loop(0, NLON, greet, 0, unroll=8)

    for f in range(NF):
        table[f] = jnp.float32(RATIO[f])
        table[32 + f] = jnp.float32(0.65 * 1.1 ** (-f))

    for cp in smalls:
        cp.wait()
    pc = pc_ref[...]
    valid = pc >= 0
    cell = jnp.maximum(pc, 0)
    col_x = cell // (GY * NLAT)
    col_y = cell % (GY * NLAT)
    owner = (col_x // GX) * NLAT + col_y // GY
    local = (col_x % GX) * GY + col_y % GY
    owner = jnp.where(valid, owner, NDEV)
    own = (lax.broadcasted_iota(jnp.int32, (NDEV, CELLS), 0) == owner).astype(F32)
    own16 = own.astype(BF16)
    upper = (
        lax.broadcasted_iota(jnp.int32, (128, 128), 0) < lax.broadcasted_iota(jnp.int32, (128, 128), 1)
    ).astype(F32).astype(BF16)
    seen = jnp.zeros((NDEV, 1), F32)
    blocks = []
    for i in range(CELLS // 128):
        part = own[:, 128 * i : 128 * (i + 1)]
        blocks.append(nn_dot(part.astype(BF16), upper) + seen)
        seen = seen + jnp.sum(part, axis=1, keepdims=True)
    before = jnp.concatenate(blocks, axis=1)
    where = jnp.sum(before * own, axis=0, keepdims=True).astype(jnp.int32)
    target = jnp.where(valid, owner * CAP + where, CELLS)
    ohs_ref[...] = (lax.broadcasted_iota(jnp.int32, (CELLS, CELLS), 0) == target).astype(F32).astype(BF16)

    wd = wd_ref[...]
    cw, sw = jnp.cos(wd), jnp.sin(wd)
    wg = wg_ref[...]
    acc = jnp.zeros((8, CELLS), F32)
    acc4 = jnp.zeros((4, CELLS), F32)
    for f in range(NF):
        if f % 5 == 0:
            loads[f // 5].wait()
        s = spec_ref[f, 0:8, :] + spec_ref[f, 8:16, :] + spec_ref[f, 16:24, :] + spec_ref[f, 24:32, :]
        acc = acc + WIDTH[f] * s
        acc4 = acc4 + WIDTH[f] * spec_ref[f, 32:36, :]
    energy = jnp.sum(acc, axis=0, keepdims=True) + jnp.sum(acc4, axis=0, keepdims=True)
    load = 0.4 * (energy / (energy + 10.0))
    for d in range(ND):
        lobe = jnp.maximum(COS[d] * cw + SIN[d] * sw, 0.0)
        r_ref[d : d + 1, :] = wg * (lobe * lobe) - load

    last_base = 36 * (NF - 1)
    v_ref[last_base : last_base + 32, :] = spec_ref[NF - 1, 0:32, :] * jnp.exp(RATIO[NF - 1] * r_ref[0:32, :])
    v_ref[last_base + 32 : last_base + 36, :] = spec_ref[NF - 1, 32:36, :] * jnp.exp(RATIO[NF - 1] * r_ref[32:36, :])

    b_ref[...] = jnp.zeros_like(b_ref)
    last = v_ref[128 * NT : 128 * NT + 4, :]
    ident = (local + 1).astype(F32)
    for s in range(CAP):
        here = (where == s).astype(F32)
        b_ref[4 * s : 4 * s + 4, :] = last * here
        b_ref[4 * CAP + s : 4 * CAP + s + 1, :] = ident * here
    bh, bl = split(b_ref[...])
    sbuf[:, 8 * NT, :] = nt_dot(own16, bh) + nt_dot(own16, bl)

    def push(rows, sem):
        pltpu.make_async_copy(sbuf.at[me, rows], rbuf.at[me, rows], sem).start()

        def go(j, carry):
            b, e, dc = lax.rem(j, 4), lax.rem(lax.div(j, 4), 4), lax.div(j, 16)
            cc = lax.rem(c + dc, 2)
            for a in range(4):
                lo = (lax.rem(y + b + a, 4) * 4 + lax.rem(z + e + a, 4)) * 2 + cc
                la = lax.rem(x + a, 4)
                copy = pltpu.make_async_remote_copy(
                    src_ref=sbuf.at[lo * NLAT + la, rows], dst_ref=rbuf.at[me, rows],
                    send_sem=send_sem, recv_sem=sem, device_id=(lo, la), device_id_type=MESH,
                )
                if a == 0:
                    pl.when(j > 0)(copy.start)
                else:
                    copy.start()
            return carry

        lax.fori_loop(0, NDEV // 4, go, 0)

    def tile(t):
        return pl.ds(pl.multiple_of(8 * t, 8), 8)

    def arrive(rows, sem):
        pltpu.make_async_copy(rbuf.at[:, rows], rbuf.at[:, rows], sem).wait()

    def grow(q, carry):
        base = pl.multiple_of(72 * q, 8)
        f, g = 2 * q, 2 * q + 1
        e4 = []
        for i, h in enumerate((f, g)):
            ratio = table[h]
            v_ref[pl.ds(base + 32 * i, 32), :] = spec_ref[h, 0:32, :] * jnp.exp(ratio * r_ref[0:32, :])
            e4.append(spec_ref[h, 32:36, :] * jnp.exp(ratio * r_ref[32:36, :]))
        v_ref[pl.ds(base + 64, 8), :] = jnp.concatenate(e4, axis=0)
        return carry

    def pairs(t):
        return jnp.where(t == 0, 0, jnp.minimum(lax.div(16 * t + 8, 9), NF // 2))

    def group(t):
        lax.fori_loop(pairs(t), pairs(t + 1), grow, 0)
        hi, lo = split(v_ref[pl.ds(pl.multiple_of(128 * t, 128), 128), :])
        both = nt_dot(ohs_ref[...], jnp.concatenate([hi, lo], axis=0))
        res = both[:, :128] + both[:, 128:]
        sbuf[:, tile(t), :] = res.reshape(NDEV, CAP, 128)

    pl.semaphore_wait(barrier, NDEV - 1)
    push(pl.ds(8 * NT, 1), recv_sem.at[NT])

    def prologue(t, carry):
        group(t)

        @pl.when(t < 3)
        def _():
            push(tile(t), recv_sem.at[t])

        return carry

    lax.fori_loop(0, 4, prologue, 0)

    sh = as_tile(sh_ref)
    sea = as_tile(mask_ref).astype(F32)
    fill_turns(turn_ref, sx_ref, sy_ref)
    lat = Lattice()
    low = (x > 0).astype(F32)
    high = (x < NLAT - 1).astype(F32)

    arrive(pl.ds(8 * NT, 1), recv_sem.at[NT])
    tail = rbuf[:, 8 * NT, :]
    ident = tail[:, 4 * CAP : 5 * CAP]
    spread = (
        lax.broadcasted_iota(jnp.int32, (CAP, CELLS), 1) % CAP == lax.broadcasted_iota(jnp.int32, (CAP, CELLS), 0)
    ).astype(F32).astype(BF16)
    ih, il = split(ident)
    wide = nn_dot(ih, spread) + nn_dot(il, spread)
    mine = lax.broadcasted_iota(jnp.int32, (NDEV, CELLS), 1) // CAP == lax.broadcasted_iota(jnp.int32, (NDEV, CELLS), 0)
    ids = jnp.sum(jnp.where(mine, wide, 0.0), axis=0, keepdims=True).astype(jnp.int32) - 1
    ohr_ref[...] = (lax.broadcasted_iota(jnp.int32, (CELLS, CELLS), 0) == ids).astype(F32).astype(BF16)
    cols = []
    th, tl = split(tail)
    for k in range(4):
        pick = (
            lax.broadcasted_iota(jnp.int32, (128, CELLS), 0) == 4 * (lax.broadcasted_iota(jnp.int32, (128, CELLS), 1) % CAP) + k
        ).astype(F32).astype(BF16)
        w = nn_dot(th, pick) + nn_dot(tl, pick)
        cols.append(jnp.sum(jnp.where(mine, w, 0.0), axis=0, keepdims=True))
    ch, cl = split(jnp.concatenate(cols + [jnp.zeros((4, CELLS), F32)], axis=0))
    tailv = nt_dot(ch, ohr_ref[...]) + nt_dot(cl, ohr_ref[...])
    for ct in range(8):
        field_ref[128 * NT : 128 * NT + 8, ct, :] = tailv[:, 128 * ct : 128 * (ct + 1)]

    def unplace(t):
        hi, lo = split(rbuf[:, tile(t), :].reshape(CELLS, 128))
        both = nn_dot(ohr_ref[...], jnp.concatenate([hi, lo], axis=1))
        res = both[:, :128] + both[:, 128:]
        for ct in range(8):
            field_ref[pl.ds(pl.multiple_of(128 * t, 128), 128), ct, :] = res[128 * ct : 128 * (ct + 1), :].T

    def faces(s, f):
        bufs = zip((up_out, dn_out, yp_out, ym_out), (up_in, dn_in, yp_in, ym_in), (nxt, prv, ynxt, yprv))
        return [
            pltpu.make_async_remote_copy(
                src_ref=src.at[s, f], dst_ref=dst.at[s, f], send_sem=face_send.at[s, n],
                recv_sem=face_recv.at[s, n, f], device_id=who, device_id_type=MESH,
            )
            for n, (src, dst, who) in enumerate(bufs)
        ]

    def send(s, f):
        for copy in faces(s, f):
            copy.start()

    def await_faces(s, f):
        for copy in faces(s, f):
            copy.wait_recv()

    def outgoing(s, f):
        return Faces(lat, up_out.at[s, f], dn_out.at[s, f], yp_out.at[s, f], ym_out.at[s, f])

    def propagate(s, f, get, put):
        await_faces(s, f)
        substep(
            lat, get, sh, sea, lambda d: turn_ref[d], table[32 + f],
            lambda k: up_in[s, f, k], lambda k: dn_in[s, f, k], yp_in[s, f] * low, ym_in[s, f] * high, put,
        )

    def over(lo, hi, fn):
        def body(f, carry):
            fn(f)
            return carry

        lax.fori_loop(lo, hi, body, 0)

    def chain(lo, hi, fn, s):
        def body(f, carry):
            fn(f)

            @pl.when(f > lo)
            def _():
                send(s, f - 1)

            return carry

        lax.fori_loop(lo, hi, body, 0)

        @pl.when(hi > lo)
        def _():
            send(s, hi - 1)

    def start_face(f):
        face = outgoing(0, f)
        for d in range(ND):
            face.put(d, sh * field_ref[row_dyn(f, d)])
        face.close()

    def first(f):
        face = outgoing(1, f)

        def put(d, v):
            f1_ref[f, d] = v
            face.put(d, sh * v)

        propagate(0, f, lambda d: field_ref[row_dyn(f, d)], put)
        face.close()

    def second(f):
        def put(d, v):
            stage_ref[f, d, pl.ds(0, 4, 2), :] = v[0:4, :]
            stage_ref[f, d, pl.ds(1, 4, 2), :] = v[4:8, :]

        propagate(1, f, lambda d: f1_ref[f, d], put)

    def emit(f):
        pltpu.make_async_copy(stage_ref.at[f], out_hbm.at[f], out_sem).start()

    def step(t, carry):
        @pl.when(t < NT)
        def _():
            arrive(tile(t), recv_sem.at[t])
            unplace(t)

        chain(whole(t), whole(t + 1), start_face, 0)

        @pl.when(t + 3 < NT)
        def _():
            push(tile(t + 3), recv_sem.at[t + 3])

        @pl.when(t + 4 < NT)
        def _():
            group(t + 4)

        chain(whole(t - 1), whole(t), first, 1)
        over(whole(t - 2), whole(t - 1), second)
        over(whole(t - 2), whole(t - 1), emit)
        return carry

    lax.fori_loop(0, NT + 2, step, 0)
    sent = sbuf.at[pl.ds(0, NDEV - 1), pl.ds(0, ROWS)]
    pltpu.make_async_copy(sent, sent, send_sem).wait()
    for s in range(2):
        for n, src in enumerate((up_out, dn_out, yp_out, ym_out)):
            pltpu.make_async_copy(src.at[s], src.at[s], face_send.at[s, n]).wait()
    pltpu.make_async_copy(stage_ref, out_hbm, out_sem).wait()


def emit_kernel(in_ref, out_ref, buf, in_sem, out_sem):
    def part(i):
        return pl.ds(5 * i, 5)

    reads = [pltpu.make_async_copy(in_ref.at[part(i)], buf.at[part(i)], in_sem.at[i]) for i in range(5)]
    writes = [pltpu.make_async_copy(buf.at[part(i)], out_ref.at[part(i)], out_sem.at[i]) for i in range(5)]
    for cp in reads:
        cp.start()
    for read, write in zip(reads, writes):
        read.wait()
        write.start()
    for cp in writes:
        cp.wait()


def on_device(spectra, wind_growth, wind_dir, point_cell, land_mask, shoaling, slope_x, slope_y):
    face = [(2, NF, PHALF, 8, 128), (2, NF, PHALF, 8, 128), (2, NF, 8, 128), (2, NF, 8, 128)]
    out = pl.pallas_call(
        step_kernel,
        out_shape=jax.ShapeDtypeStruct((NF, ND, 8, 128), F32),
        in_specs=[pl.BlockSpec(memory_space=pl.ANY)] * 8,
        out_specs=pl.BlockSpec(memory_space=pl.ANY),
        scratch_shapes=[
            pltpu.VMEM((1, CELLS), F32),
            pltpu.VMEM((1, CELLS), F32),
            pltpu.VMEM((1, CELLS), jnp.int32),
            pltpu.VMEM((GX, GY), jnp.int32),
            pltpu.VMEM((GX, GY), F32),
            pltpu.VMEM((GX, GY), F32),
            pltpu.VMEM((GX, GY), F32),
            pltpu.VMEM((NF, ND, CELLS), F32),
            pltpu.VMEM((40, CELLS), F32),
            pltpu.VMEM((904, CELLS), F32),
            pltpu.VMEM((128, CELLS), F32),
            pltpu.VMEM((NDEV, 64, 128), F32),
            pltpu.VMEM((NDEV, 64, 128), F32),
            pltpu.VMEM((CELLS, CELLS), BF16),
            pltpu.VMEM((CELLS, CELLS), BF16),
            pltpu.VMEM((904, 8, 128), F32),
            pltpu.VMEM((NF, ND, 8, 128), F32),
            pltpu.VMEM((NF, ND, 8, 128), F32),
            pltpu.VMEM((ND, 8, 128), F32),
        ]
        + [pltpu.VMEM(s, F32) for s in face] * 2
        + [
            pltpu.SMEM((64,), F32),
            pltpu.SemaphoreType.DMA((7,)),
            pltpu.SemaphoreType.DMA((5,)),
            pltpu.SemaphoreType.DMA,
            pltpu.SemaphoreType.DMA((NT + 1,)),
            pltpu.SemaphoreType.DMA((2, 4)),
            pltpu.SemaphoreType.DMA((2, 4, NF)),
            pltpu.SemaphoreType.DMA,
        ],
        compiler_params=pltpu.CompilerParams(collective_id=0, has_side_effects=True, vmem_limit_bytes=VMEM_LIMIT),
        name="wave_step",
    )(
        spectra, wind_growth.reshape(1, CELLS), wind_dir.reshape(1, CELLS), point_cell.reshape(1, CELLS),
        land_mask, shoaling, slope_x, slope_y,
    )
    out = pl.pallas_call(
        emit_kernel,
        out_shape=jax.ShapeDtypeStruct((NF, ND, 8, 128), F32),
        in_specs=[pl.BlockSpec(memory_space=pl.ANY)],
        out_specs=pl.BlockSpec(memory_space=pl.ANY),
        scratch_shapes=[
            pltpu.VMEM((NF, ND, 8, 128), F32),
            pltpu.SemaphoreType.DMA((5,)),
            pltpu.SemaphoreType.DMA((5,)),
        ],
        compiler_params=pltpu.CompilerParams(vmem_limit_bytes=VMEM_LIMIT),
        name="emit",
    )(out)
    out = out.reshape(NF, ND, 4, GX, 128)
    return jnp.transpose(out, (0, 1, 3, 2, 4)).reshape(NF, ND, GX, GY)


def solution(mesh):
    placed = (
        P(None, None, ("lon", "lat")),
        P(("lon", "lat")),
        P(("lon", "lat")),
        P(("lon", "lat")),
        P("lon", "lat"),
        P("lon", "lat"),
        P("lon", "lat"),
        P("lon", "lat"),
    )
    return jax.shard_map(
        on_device, mesh=mesh, in_specs=placed, out_specs=P(None, None, "lon", "lat"), check_vma=False
    )
```

```python
import functools
import math

import jax
import jax.numpy as jnp
from jax import lax
from jax.experimental import pallas as pl
from jax.experimental.pallas import tpu as pltpu
from jax.sharding import PartitionSpec as P

MESH = pl.DeviceIdType.MESH
F32 = jnp.float32
BF16 = jnp.bfloat16

NF, ND = 25, 36
GX, GY = 2, 512
NLON, NLAT = 32, 4
NDEV = NLON * NLAT
CELLS = GX * GY
CAP = CELLS // NDEV
NT = 7
ROWS = 57
DTH = 2.0 * math.pi / ND
THETA = [(d + 0.5) * DTH for d in range(ND)]
COS = [math.cos(t) for t in THETA]
SIN = [math.sin(t) for t in THETA]
RATIO = [1.1 ** (f - (NF - 1)) for f in range(NF)]
WIDTH = [0.1 * 1.1**f * DTH for f in range(NF)]
CPLUS = [d for d in range(27, 36)] + [d for d in range(0, 9)]
CMINUS = [d for d in range(9, 27)]
SPLUS = list(range(0, 18))
SMINUS = list(range(18, 36))
PHALF = 9
VMEM_LIMIT = 60 << 20


def row_of(f, d):
    if f == NF - 1:
        return 36 * (NF - 1) + d
    base = 72 * (f // 2)
    if d < 32:
        return base + 32 * (f % 2) + d
    return base + 64 + 4 * (f % 2) + (d - 32)


def row_dyn(f, d):
    base = 72 * lax.div(f, 2)
    if d < 32:
        return base + 32 * lax.rem(f, 2) + d
    return base + jnp.where(f == NF - 1, 32, 64 + 4 * lax.rem(f, 2)) + (d - 32)


def whole(t):
    t = jnp.clip(t, 0, NT)
    return 2 * lax.div(16 * t, 9) + lax.div(t, NT)


def split(v):
    hi = v.astype(BF16)
    lo = (v - hi.astype(F32)).astype(BF16)
    return hi, lo


def nt_dot(a, b):
    return lax.dot_general(a, b, (((1,), (1,)), ((), ())), preferred_element_type=F32)


def nn_dot(a, b):
    return lax.dot_general(a, b, (((1,), (0,)), ((), ())), preferred_element_type=F32)


def as_tile(ref):
    return jnp.concatenate([ref[i : i + 1, 128 * j : 128 * (j + 1)] for i in range(GX) for j in range(4)], axis=0)


class Lattice:
    def __init__(self):
        sub = lax.broadcasted_iota(jnp.int32, (8, 128), 0)
        lane = lax.broadcasted_iota(jnp.int32, (8, 128), 1)
        self.lane = lane
        self.upper = sub >= 4
        self.lane0 = lane == 0
        self.lane127 = lane == 127
        self.first = (sub % 4 == 0) & self.lane0
        self.last = (sub % 4 == 3) & self.lane127
        self.lane0 = self.lane0 & (sub % 4 != 0)
        self.lane127 = self.lane127 & (sub % 4 != 3)


def lanes(v, k):
    return v if k % 128 == 0 else pltpu.roll(v, k % 128, 1)


def subs(v, k):
    return v if k % 8 == 0 else pltpu.roll(v, k % 8, 0)


class Faces:
    def __init__(self, lat, up_ref, dn_ref, yp_ref, ym_ref):
        self.lat, self.up, self.dn, self.yp_ref, self.ym_ref = lat, up_ref, dn_ref, yp_ref, ym_ref
        self.yp = jnp.zeros((8, 128), F32)
        self.ym = jnp.zeros((8, 128), F32)

    def put(self, d, g):
        if d in CPLUS:
            k = CPLUS.index(d)
            if k < PHALF:
                self.up[k, 4:8, :] = g[4:8, :]
            else:
                self.up[k - PHALF, 0:4, :] = g[4:8, :]
        else:
            k = CMINUS.index(d)
            if k < PHALF:
                self.dn[k, 0:4, :] = g[0:4, :]
            else:
                self.dn[k - PHALF, 4:8, :] = g[0:4, :]
        if d in SPLUS:
            k = SPLUS.index(d)
            self.yp = jnp.where(self.lat.lane == k, lanes(g, k + 1), self.yp)
        else:
            k = SMINUS.index(d)
            self.ym = jnp.where(self.lat.lane == k, lanes(g, k), self.ym)

    def close(self):
        self.yp_ref[...] = self.yp
        self.ym_ref[...] = self.ym


def substep(lat, field, sh, sea, turns, speed, up, dn, yp, ym, put):
    yp = subs(yp, 5)
    ym = subs(ym, 3)

    def moved(d):
        v = field(d)
        g = sh * v
        if d in CPLUS:
            k = CPLUS.index(d)
            if k < PHALF:
                gx = subs(jnp.where(lat.upper, up(k), g), 4)
            else:
                gx = jnp.where(lat.upper, subs(g, 4), up(k - PHALF))
        else:
            k = CMINUS.index(d)
            if k < PHALF:
                gx = subs(jnp.where(lat.upper, g, dn(k)), 4)
            else:
                gx = jnp.where(lat.upper, dn(k - PHALF), subs(g, 4))
        if d in SPLUS:
            k = SPLUS.index(d)
            r = lanes(g, 1)
            gy = jnp.where(lat.lane0, subs(r, 1), r)
            gy = jnp.where(lat.first, lanes(yp, -k), gy)
        else:
            k = SMINUS.index(d)
            r = lanes(g, 127)
            gy = jnp.where(lat.lane127, subs(r, 7), r)
            gy = jnp.where(lat.last, lanes(ym, 127 - k), gy)
        h = v - (speed * abs(COS[d])) * (g - gx) - (speed * abs(SIN[d])) * (g - gy)
        qt = (speed * turns(d)) * h
        return h, jnp.maximum(qt, 0.0), jnp.minimum(qt, 0.0)

    begin = moved(0)
    end = moved(ND - 1)
    west, here = end, begin
    for d in range(ND):
        east = begin if d == ND - 1 else (end if d == ND - 2 else moved(d + 1))
        put(d, (here[0] - (here[1] + east[2]) + (west[1] + here[2])) * sea)
        west, here = here, east


def fill_turns(turn_ref, sx_ref, sy_ref):
    sx, sy = as_tile(sx_ref), as_tile(sy_ref)
    for d in range(ND):
        turn_ref[d] = SIN[d] * sx - COS[d] * sy


def step_kernel(
    spec_hbm, wg_hbm, wd_hbm, pc_hbm, mask_hbm, sh_hbm, sx_hbm, sy_hbm, out_hbm,
    wg_ref, wd_ref, pc_ref, mask_ref, sh_ref, sx_ref, sy_ref,
    spec_ref, r_ref, v_ref, b_ref, sbuf, rbuf, ohs_ref, ohr_ref, field_ref, f1_ref, stage_ref, turn_ref,
    up_out, dn_out, yp_out, ym_out, up_in, dn_in, yp_in, ym_in, table,
    small_sem, spec_sem, send_sem, recv_sem, face_send, face_recv, out_sem,
):
    lon = lax.axis_index("lon")
    x = lax.axis_index("lat")
    me = lon * NLAT + x
    c = lax.rem(lon, 2)
    z = lax.rem(lax.div(lon, 2), 4)
    y = lax.div(lon, 8)
    nxt = (lax.rem(lon + 1, NLON), x)
    prv = (lax.rem(lon + NLON - 1, NLON), x)
    ynxt = (lon, lax.rem(x + 1, NLAT))
    yprv = (lon, lax.rem(x + NLAT - 1, NLAT))

    barrier = pltpu.get_barrier_semaphore()
    columns = [lax.rem(x + a, NLAT) for a in range(NLAT)]

    def greet(k, carry):
        row = lax.rem(lon + k, NLON)
        for a in range(NLAT):
            signal = functools.partial(
                pl.semaphore_signal, barrier, 1, device_id=(row, columns[a]), device_id_type=MESH
            )
            if a == 0:
                pl.when(k > 0)(signal)
            else:
                signal()
        return carry

    smalls = [
        pltpu.make_async_copy(src, dst, small_sem.at[n])
        for n, (src, dst) in enumerate(
            (
                (pc_hbm, pc_ref), (wd_hbm, wd_ref), (wg_hbm, wg_ref), (mask_hbm, mask_ref),
                (sh_hbm, sh_ref), (sx_hbm, sx_ref), (sy_hbm, sy_ref),
            )
        )
    ]
    for cp in smalls:
        cp.start()
    loads = [
        pltpu.make_async_copy(spec_hbm.at[pl.ds(5 * i, 5)], spec_ref.at[pl.ds(5 * i, 5)], spec_sem.at[i])
        for i in range(5)
    ]
    for cp in loads:
        cp.start()
    lax.fori_loop(0, NLON, greet, 0, unroll=8)

    for f in range(NF):
        table[f] = jnp.float32(RATIO[f])
        table[32 + f] = jnp.float32(0.65 * 1.1 ** (-f))

    for cp in smalls:
        cp.wait()
    pc = pc_ref[...]
    valid = pc >= 0
    cell = jnp.maximum(pc, 0)
    col_x = cell // (GY * NLAT)
    col_y = cell % (GY * NLAT)
    owner = (col_x // GX) * NLAT + col_y // GY
    local = (col_x % GX) * GY + col_y % GY
    owner = jnp.where(valid, owner, NDEV)
    own = (lax.broadcasted_iota(jnp.int32, (NDEV, CELLS), 0) == owner).astype(F32)
    own16 = own.astype(BF16)
    upper = (
        lax.broadcasted_iota(jnp.int32, (128, 128), 0) < lax.broadcasted_iota(jnp.int32, (128, 128), 1)
    ).astype(F32).astype(BF16)
    seen = jnp.zeros((NDEV, 1), F32)
    blocks = []
    for i in range(CELLS // 128):
        part = own[:, 128 * i : 128 * (i + 1)]
        blocks.append(nn_dot(part.astype(BF16), upper) + seen)
        seen = seen + jnp.sum(part, axis=1, keepdims=True)
    before = jnp.concatenate(blocks, axis=1)
    where = jnp.sum(before * own, axis=0, keepdims=True).astype(jnp.int32)
    target = jnp.where(valid, owner * CAP + where, CELLS)
    ohs_ref[...] = (lax.broadcasted_iota(jnp.int32, (CELLS, CELLS), 0) == target).astype(F32).astype(BF16)

    wd = wd_ref[...]
    cw, sw = jnp.cos(wd), jnp.sin(wd)
    wg = wg_ref[...]
    acc = jnp.zeros((8, CELLS), F32)
    acc4 = jnp.zeros((4, CELLS), F32)
    for f in range(NF):
        if f % 5 == 0:
            loads[f // 5].wait()
        s = spec_ref[f, 0:8, :] + spec_ref[f, 8:16, :] + spec_ref[f, 16:24, :] + spec_ref[f, 24:32, :]
        acc = acc + WIDTH[f] * s
        acc4 = acc4 + WIDTH[f] * spec_ref[f, 32:36, :]
    energy = jnp.sum(acc, axis=0, keepdims=True) + jnp.sum(acc4, axis=0, keepdims=True)
    load = 0.4 * (energy / (energy + 10.0))
    for d in range(ND):
        lobe = jnp.maximum(COS[d] * cw + SIN[d] * sw, 0.0)
        r_ref[d : d + 1, :] = wg * (lobe * lobe) - load

    last_base = 36 * (NF - 1)
    v_ref[last_base : last_base + 32, :] = spec_ref[NF - 1, 0:32, :] * jnp.exp(RATIO[NF - 1] * r_ref[0:32, :])
    v_ref[last_base + 32 : last_base + 36, :] = spec_ref[NF - 1, 32:36, :] * jnp.exp(RATIO[NF - 1] * r_ref[32:36, :])

    b_ref[...] = jnp.zeros_like(b_ref)
    last = v_ref[128 * NT : 128 * NT + 4, :]
    ident = (local + 1).astype(F32)
    for s in range(CAP):
        here = (where == s).astype(F32)
        b_ref[4 * s : 4 * s + 4, :] = last * here
        b_ref[4 * CAP + s : 4 * CAP + s + 1, :] = ident * here
    bh, bl = split(b_ref[...])
    sbuf[:, 8, :] = nt_dot(own16, bh) + nt_dot(own16, bl)

    def push(rows, sem):
        pltpu.make_async_copy(sbuf.at[me, rows], rbuf.at[me, rows], sem).start()

        def go(j, carry):
            b, e, dc = lax.rem(j, 4), lax.rem(lax.div(j, 4), 4), lax.div(j, 16)
            cc = lax.rem(c + dc, 2)
            for a in range(4):
                lo = (lax.rem(y + b + a, 4) * 4 + lax.rem(z + e + a, 4)) * 2 + cc
                la = lax.rem(x + a, 4)
                copy = pltpu.make_async_remote_copy(
                    src_ref=sbuf.at[lo * NLAT + la, rows], dst_ref=rbuf.at[me, rows],
                    send_sem=send_sem, recv_sem=sem, device_id=(lo, la), device_id_type=MESH,
                )
                if a == 0:
                    pl.when(j > 0)(copy.start)
                else:
                    copy.start()
            return carry

        lax.fori_loop(0, NDEV // 4, go, 0)

    def tile(t):
        return pl.ds(pl.multiple_of(8 * (t + jnp.minimum(t, 1)), 8), 8)

    front = pl.ds(0, 9)

    def arrive(rows, sem):
        pltpu.make_async_copy(rbuf.at[:, rows], rbuf.at[:, rows], sem).wait()

    def grow(q, carry):
        base = pl.multiple_of(72 * q, 8)
        f, g = 2 * q, 2 * q + 1
        e4 = []
        for i, h in enumerate((f, g)):
            ratio = table[h]
            v_ref[pl.ds(base + 32 * i, 32), :] = spec_ref[h, 0:32, :] * jnp.exp(ratio * r_ref[0:32, :])
            e4.append(spec_ref[h, 32:36, :] * jnp.exp(ratio * r_ref[32:36, :]))
        v_ref[pl.ds(base + 64, 8), :] = jnp.concatenate(e4, axis=0)
        return carry

    def pairs(t):
        return jnp.where(t == 0, 0, jnp.minimum(lax.div(16 * t + 8, 9), NF // 2))

    def group(t):
        lax.fori_loop(pairs(t), pairs(t + 1), grow, 0)
        hi, lo = split(v_ref[pl.ds(pl.multiple_of(128 * t, 128), 128), :])
        both = nt_dot(ohs_ref[...], jnp.concatenate([hi, lo], axis=0))
        res = both[:, :128] + both[:, 128:]
        sbuf[:, tile(t), :] = res.reshape(NDEV, CAP, 128)

    group(jnp.int32(0))
    pl.semaphore_wait(barrier, NDEV - 1)
    push(front, recv_sem.at[0])

    def prologue(t, carry):
        group(t)

        @pl.when(t < 3)
        def _():
            push(tile(t), recv_sem.at[t])

        return carry

    lax.fori_loop(1, 4, prologue, 0)

    sh = as_tile(sh_ref)
    sea = as_tile(mask_ref).astype(F32)
    fill_turns(turn_ref, sx_ref, sy_ref)
    lat = Lattice()
    low = (x > 0).astype(F32)
    high = (x < NLAT - 1).astype(F32)

    arrive(front, recv_sem.at[0])
    tail = rbuf[:, 8, :]
    ident = tail[:, 4 * CAP : 5 * CAP]
    spread = (
        lax.broadcasted_iota(jnp.int32, (CAP, CELLS), 1) % CAP == lax.broadcasted_iota(jnp.int32, (CAP, CELLS), 0)
    ).astype(F32).astype(BF16)
    ih, il = split(ident)
    wide = nn_dot(ih, spread) + nn_dot(il, spread)
    mine = lax.broadcasted_iota(jnp.int32, (NDEV, CELLS), 1) // CAP == lax.broadcasted_iota(jnp.int32, (NDEV, CELLS), 0)
    ids = jnp.sum(jnp.where(mine, wide, 0.0), axis=0, keepdims=True).astype(jnp.int32) - 1
    ohr_ref[...] = (lax.broadcasted_iota(jnp.int32, (CELLS, CELLS), 0) == ids).astype(F32).astype(BF16)
    cols = []
    th, tl = split(tail)
    for k in range(4):
        pick = (
            lax.broadcasted_iota(jnp.int32, (128, CELLS), 0) == 4 * (lax.broadcasted_iota(jnp.int32, (128, CELLS), 1) % CAP) + k
        ).astype(F32).astype(BF16)
        w = nn_dot(th, pick) + nn_dot(tl, pick)
        cols.append(jnp.sum(jnp.where(mine, w, 0.0), axis=0, keepdims=True))
    ch, cl = split(jnp.concatenate(cols + [jnp.zeros((4, CELLS), F32)], axis=0))
    tailv = nt_dot(ch, ohr_ref[...]) + nt_dot(cl, ohr_ref[...])
    for ct in range(8):
        field_ref[128 * NT : 128 * NT + 8, ct, :] = tailv[:, 128 * ct : 128 * (ct + 1)]

    def unplace(t):
        hi, lo = split(rbuf[:, tile(t), :].reshape(CELLS, 128))
        both = nn_dot(ohr_ref[...], jnp.concatenate([hi, lo], axis=1))
        res = both[:, :128] + both[:, 128:]
        for ct in range(8):
            field_ref[pl.ds(pl.multiple_of(128 * t, 128), 128), ct, :] = res[128 * ct : 128 * (ct + 1), :].T

    def faces(s, f):
        bufs = zip((up_out, dn_out, yp_out, ym_out), (up_in, dn_in, yp_in, ym_in), (nxt, prv, ynxt, yprv))
        return [
            pltpu.make_async_remote_copy(
                src_ref=src.at[s, f], dst_ref=dst.at[s, f], send_sem=face_send.at[s, n],
                recv_sem=face_recv.at[s, n, f], device_id=who, device_id_type=MESH,
            )
            for n, (src, dst, who) in enumerate(bufs)
        ]

    def send(s, f):
        for copy in faces(s, f):
            copy.start()

    def await_faces(s, f):
        for copy in faces(s, f):
            copy.wait_recv()

    def outgoing(s, f):
        return Faces(lat, up_out.at[s, f], dn_out.at[s, f], yp_out.at[s, f], ym_out.at[s, f])

    def propagate(s, f, get, put):
        await_faces(s, f)
        substep(
            lat, get, sh, sea, lambda d: turn_ref[d], table[32 + f],
            lambda k: up_in[s, f, k], lambda k: dn_in[s, f, k], yp_in[s, f] * low, ym_in[s, f] * high, put,
        )

    def over(lo, hi, fn):
        def body(f, carry):
            fn(f)
            return carry

        lax.fori_loop(lo, hi, body, 0)

    def chain(lo, hi, fn, s):
        def body(f, carry):
            fn(f)

            @pl.when(f > lo)
            def _():
                send(s, f - 1)

            return carry

        lax.fori_loop(lo, hi, body, 0)

        @pl.when(hi > lo)
        def _():
            send(s, hi - 1)

    def start_face(f):
        face = outgoing(0, f)
        for d in range(ND):
            face.put(d, sh * field_ref[row_dyn(f, d)])
        face.close()

    def first(f):
        face = outgoing(1, f)

        def put(d, v):
            f1_ref[f, d] = v
            face.put(d, sh * v)

        propagate(0, f, lambda d: field_ref[row_dyn(f, d)], put)
        face.close()

    def second(f):
        def put(d, v):
            stage_ref[f, d, pl.ds(0, 4, 2), :] = v[0:4, :]
            stage_ref[f, d, pl.ds(1, 4, 2), :] = v[4:8, :]

        propagate(1, f, lambda d: f1_ref[f, d], put)

    def emit(f):
        pltpu.make_async_copy(stage_ref.at[f], out_hbm.at[f], out_sem).start()

    def step(t, carry):
        @pl.when((t > 0) & (t < NT))
        def _():
            arrive(tile(t), recv_sem.at[t])

        @pl.when(t < NT)
        def _():
            unplace(t)

        chain(whole(t), whole(t + 1), start_face, 0)

        @pl.when(t + 3 < NT)
        def _():
            push(tile(t + 3), recv_sem.at[t + 3])

        @pl.when(t + 4 < NT)
        def _():
            group(t + 4)

        chain(whole(t - 1), whole(t), first, 1)
        over(whole(t - 2), whole(t - 1), second)
        over(whole(t - 2), whole(t - 1), emit)
        return carry

    lax.fori_loop(0, NT + 2, step, 0)
    sent = sbuf.at[pl.ds(0, NDEV - 1), pl.ds(0, ROWS)]
    pltpu.make_async_copy(sent, sent, send_sem).wait()
    for s in range(2):
        for n, src in enumerate((up_out, dn_out, yp_out, ym_out)):
            pltpu.make_async_copy(src.at[s], src.at[s], face_send.at[s, n]).wait()
    pltpu.make_async_copy(stage_ref, out_hbm, out_sem).wait()


def emit_kernel(in_ref, out_ref, buf, in_sem, out_sem):
    def part(i):
        return pl.ds(5 * i, 5)

    reads = [pltpu.make_async_copy(in_ref.at[part(i)], buf.at[part(i)], in_sem.at[i]) for i in range(5)]
    writes = [pltpu.make_async_copy(buf.at[part(i)], out_ref.at[part(i)], out_sem.at[i]) for i in range(5)]
    for cp in reads:
        cp.start()
    for read, write in zip(reads, writes):
        read.wait()
        write.start()
    for cp in writes:
        cp.wait()


def on_device(spectra, wind_growth, wind_dir, point_cell, land_mask, shoaling, slope_x, slope_y):
    face = [(2, NF, PHALF, 8, 128), (2, NF, PHALF, 8, 128), (2, NF, 8, 128), (2, NF, 8, 128)]
    out = pl.pallas_call(
        step_kernel,
        out_shape=jax.ShapeDtypeStruct((NF, ND, 8, 128), F32),
        in_specs=[pl.BlockSpec(memory_space=pl.ANY)] * 8,
        out_specs=pl.BlockSpec(memory_space=pl.ANY),
        scratch_shapes=[
            pltpu.VMEM((1, CELLS), F32),
            pltpu.VMEM((1, CELLS), F32),
            pltpu.VMEM((1, CELLS), jnp.int32),
            pltpu.VMEM((GX, GY), jnp.int32),
            pltpu.VMEM((GX, GY), F32),
            pltpu.VMEM((GX, GY), F32),
            pltpu.VMEM((GX, GY), F32),
            pltpu.VMEM((NF, ND, CELLS), F32),
            pltpu.VMEM((40, CELLS), F32),
            pltpu.VMEM((904, CELLS), F32),
            pltpu.VMEM((128, CELLS), F32),
            pltpu.VMEM((NDEV, 64, 128), F32),
            pltpu.VMEM((NDEV, 64, 128), F32),
            pltpu.VMEM((CELLS, CELLS), BF16),
            pltpu.VMEM((CELLS, CELLS), BF16),
            pltpu.VMEM((904, 8, 128), F32),
            pltpu.VMEM((NF, ND, 8, 128), F32),
            pltpu.VMEM((NF, ND, 8, 128), F32),
            pltpu.VMEM((ND, 8, 128), F32),
        ]
        + [pltpu.VMEM(s, F32) for s in face] * 2
        + [
            pltpu.SMEM((64,), F32),
            pltpu.SemaphoreType.DMA((7,)),
            pltpu.SemaphoreType.DMA((5,)),
            pltpu.SemaphoreType.DMA,
            pltpu.SemaphoreType.DMA((NT,)),
            pltpu.SemaphoreType.DMA((2, 4)),
            pltpu.SemaphoreType.DMA((2, 4, NF)),
            pltpu.SemaphoreType.DMA,
        ],
        compiler_params=pltpu.CompilerParams(collective_id=0, has_side_effects=True, vmem_limit_bytes=VMEM_LIMIT),
        name="wave_step",
    )(
        spectra, wind_growth.reshape(1, CELLS), wind_dir.reshape(1, CELLS), point_cell.reshape(1, CELLS),
        land_mask, shoaling, slope_x, slope_y,
    )
    out = pl.pallas_call(
        emit_kernel,
        out_shape=jax.ShapeDtypeStruct((NF, ND, 8, 128), F32),
        in_specs=[pl.BlockSpec(memory_space=pl.ANY)],
        out_specs=pl.BlockSpec(memory_space=pl.ANY),
        scratch_shapes=[
            pltpu.VMEM((NF, ND, 8, 128), F32),
            pltpu.SemaphoreType.DMA((5,)),
            pltpu.SemaphoreType.DMA((5,)),
        ],
        compiler_params=pltpu.CompilerParams(vmem_limit_bytes=VMEM_LIMIT),
        name="emit",
    )(out)
    out = out.reshape(NF, ND, 4, GX, 128)
    return jnp.transpose(out, (0, 1, 3, 2, 4)).reshape(NF, ND, GX, GY)


def solution(mesh):
    placed = (
        P(None, None, ("lon", "lat")),
        P(("lon", "lat")),
        P(("lon", "lat")),
        P(("lon", "lat")),
        P("lon", "lat"),
        P("lon", "lat"),
        P("lon", "lat"),
        P("lon", "lat"),
    )
    return jax.shard_map(
        on_device, mesh=mesh, in_specs=placed, out_specs=P(None, None, "lon", "lat"), check_vma=False
    )
```

```python
import functools
import math

import jax
import jax.numpy as jnp
from jax import lax
from jax.experimental import pallas as pl
from jax.experimental.pallas import tpu as pltpu
from jax.sharding import PartitionSpec as P

MESH = pl.DeviceIdType.MESH
F32 = jnp.float32
BF16 = jnp.bfloat16

NF, ND = 25, 36
GX, GY = 2, 512
NLON, NLAT = 32, 4
NDEV = NLON * NLAT
CELLS = GX * GY
CAP = CELLS // NDEV
NT = 7
ROWS = 57
DTH = 2.0 * math.pi / ND
THETA = [(d + 0.5) * DTH for d in range(ND)]
COS = [math.cos(t) for t in THETA]
SIN = [math.sin(t) for t in THETA]
RATIO = [1.1 ** (f - (NF - 1)) for f in range(NF)]
WIDTH = [0.1 * 1.1**f * DTH for f in range(NF)]
CPLUS = [d for d in range(27, 36)] + [d for d in range(0, 9)]
CMINUS = [d for d in range(9, 27)]
SPLUS = list(range(0, 18))
SMINUS = list(range(18, 36))
PHALF = 9
VMEM_LIMIT = 60 << 20


def row_of(f, d):
    if f == NF - 1:
        return 36 * (NF - 1) + d
    base = 72 * (f // 2)
    if d < 32:
        return base + 32 * (f % 2) + d
    return base + 64 + 4 * (f % 2) + (d - 32)


def row_dyn(f, d):
    base = 72 * lax.div(f, 2)
    if d < 32:
        return base + 32 * lax.rem(f, 2) + d
    return base + jnp.where(f == NF - 1, 32, 64 + 4 * lax.rem(f, 2)) + (d - 32)


def whole(t):
    t = jnp.clip(t, 0, NT)
    return 2 * lax.div(16 * t, 9) + lax.div(t, NT)


def split(v):
    hi = v.astype(BF16)
    lo = (v - hi.astype(F32)).astype(BF16)
    return hi, lo


def nt_dot(a, b):
    return lax.dot_general(a, b, (((1,), (1,)), ((), ())), preferred_element_type=F32)


def nn_dot(a, b):
    return lax.dot_general(a, b, (((1,), (0,)), ((), ())), preferred_element_type=F32)


def as_tile(ref):
    return jnp.concatenate([ref[i : i + 1, 128 * j : 128 * (j + 1)] for i in range(GX) for j in range(4)], axis=0)


class Lattice:
    def __init__(self):
        sub = lax.broadcasted_iota(jnp.int32, (8, 128), 0)
        lane = lax.broadcasted_iota(jnp.int32, (8, 128), 1)
        self.lane = lane
        self.upper = sub >= 4
        self.lane0 = lane == 0
        self.lane127 = lane == 127
        self.first = (sub % 4 == 0) & self.lane0
        self.last = (sub % 4 == 3) & self.lane127
        self.lane0 = self.lane0 & (sub % 4 != 0)
        self.lane127 = self.lane127 & (sub % 4 != 3)


def lanes(v, k):
    return v if k % 128 == 0 else pltpu.roll(v, k % 128, 1)


def subs(v, k):
    return v if k % 8 == 0 else pltpu.roll(v, k % 8, 0)


class Faces:
    def __init__(self, lat, up_ref, dn_ref, yp_ref, ym_ref):
        self.lat, self.up, self.dn, self.yp_ref, self.ym_ref = lat, up_ref, dn_ref, yp_ref, ym_ref
        self.yp = jnp.zeros((8, 128), F32)
        self.ym = jnp.zeros((8, 128), F32)

    def put(self, d, g):
        if d in CPLUS:
            k = CPLUS.index(d)
            if k < PHALF:
                self.up[k, 4:8, :] = g[4:8, :]
            else:
                self.up[k - PHALF, 0:4, :] = g[4:8, :]
        else:
            k = CMINUS.index(d)
            if k < PHALF:
                self.dn[k, 0:4, :] = g[0:4, :]
            else:
                self.dn[k - PHALF, 4:8, :] = g[0:4, :]
        if d in SPLUS:
            k = SPLUS.index(d)
            self.yp = jnp.where(self.lat.lane == k, lanes(g, k + 1), self.yp)
        else:
            k = SMINUS.index(d)
            self.ym = jnp.where(self.lat.lane == k, lanes(g, k), self.ym)

    def close(self):
        self.yp_ref[...] = self.yp
        self.ym_ref[...] = self.ym


def substep(lat, field, sh, sea, turns, speed, up, dn, yp, ym, put):
    yp = subs(yp, 5)
    ym = subs(ym, 3)

    def moved(d):
        v = field(d)
        g = sh * v
        if d in CPLUS:
            k = CPLUS.index(d)
            if k < PHALF:
                gx = subs(jnp.where(lat.upper, up(k), g), 4)
            else:
                gx = jnp.where(lat.upper, subs(g, 4), up(k - PHALF))
        else:
            k = CMINUS.index(d)
            if k < PHALF:
                gx = subs(jnp.where(lat.upper, g, dn(k)), 4)
            else:
                gx = jnp.where(lat.upper, dn(k - PHALF), subs(g, 4))
        if d in SPLUS:
            k = SPLUS.index(d)
            r = lanes(g, 1)
            gy = jnp.where(lat.lane0, subs(r, 1), r)
            gy = jnp.where(lat.first, lanes(yp, -k), gy)
        else:
            k = SMINUS.index(d)
            r = lanes(g, 127)
            gy = jnp.where(lat.lane127, subs(r, 7), r)
            gy = jnp.where(lat.last, lanes(ym, 127 - k), gy)
        h = v - (speed * abs(COS[d])) * (g - gx) - (speed * abs(SIN[d])) * (g - gy)
        qt = (speed * turns(d)) * h
        return h, jnp.maximum(qt, 0.0), jnp.minimum(qt, 0.0)

    begin = moved(0)
    end = moved(ND - 1)
    west, here = end, begin
    for d in range(ND):
        east = begin if d == ND - 1 else (end if d == ND - 2 else moved(d + 1))
        put(d, (here[0] - (here[1] + east[2]) + (west[1] + here[2])) * sea)
        west, here = here, east


def fill_turns(turn_ref, sx_ref, sy_ref):
    sx, sy = as_tile(sx_ref), as_tile(sy_ref)
    for d in range(ND):
        turn_ref[d] = SIN[d] * sx - COS[d] * sy


def step_kernel(
    spec_hbm, wg_hbm, wd_hbm, pc_hbm, mask_hbm, sh_hbm, sx_hbm, sy_hbm, out_hbm,
    wg_ref, wd_ref, pc_ref, mask_ref, sh_ref, sx_ref, sy_ref,
    spec_ref, r_ref, v_ref, b_ref, sbuf, rbuf, ohs_ref, ohr_ref, field_ref, f1_ref, stage_ref, turn_ref,
    up_out, dn_out, yp_out, ym_out, up_in, dn_in, yp_in, ym_in, table,
    small_sem, spec_sem, send_sem, recv_sem, face_send, face_recv, out_sem,
):
    lon = lax.axis_index("lon")
    x = lax.axis_index("lat")
    me = lon * NLAT + x
    c = lax.rem(lon, 2)
    z = lax.rem(lax.div(lon, 2), 4)
    y = lax.div(lon, 8)
    nxt = (lax.rem(lon + 1, NLON), x)
    prv = (lax.rem(lon + NLON - 1, NLON), x)
    ynxt = (lon, lax.rem(x + 1, NLAT))
    yprv = (lon, lax.rem(x + NLAT - 1, NLAT))

    barrier = pltpu.get_barrier_semaphore()
    columns = [lax.rem(x + a, NLAT) for a in range(NLAT)]

    def greet(k, carry):
        row = lax.rem(lon + k, NLON)
        for a in range(NLAT):
            signal = functools.partial(
                pl.semaphore_signal, barrier, 1, device_id=(row, columns[a]), device_id_type=MESH
            )
            if a == 0:
                pl.when(k > 0)(signal)
            else:
                signal()
        return carry

    smalls = [
        pltpu.make_async_copy(src, dst, small_sem.at[n])
        for n, (src, dst) in enumerate(
            (
                (pc_hbm, pc_ref), (wd_hbm, wd_ref), (wg_hbm, wg_ref), (mask_hbm, mask_ref),
                (sh_hbm, sh_ref), (sx_hbm, sx_ref), (sy_hbm, sy_ref),
            )
        )
    ]
    for cp in smalls:
        cp.start()
    loads = [
        pltpu.make_async_copy(spec_hbm.at[pl.ds(5 * i, 5)], spec_ref.at[pl.ds(5 * i, 5)], spec_sem.at[i])
        for i in range(5)
    ]
    for cp in loads:
        cp.start()
    lax.fori_loop(0, NLON, greet, 0, unroll=32)

    for f in range(NF):
        table[f] = jnp.float32(RATIO[f])
        table[32 + f] = jnp.float32(0.65 * 1.1 ** (-f))

    for cp in smalls:
        cp.wait()
    pc = pc_ref[...]
    valid = pc >= 0
    cell = jnp.maximum(pc, 0)
    col_x = cell // (GY * NLAT)
    col_y = cell % (GY * NLAT)
    owner = (col_x // GX) * NLAT + col_y // GY
    local = (col_x % GX) * GY + col_y % GY
    owner = jnp.where(valid, owner, NDEV)
    own = (lax.broadcasted_iota(jnp.int32, (NDEV, CELLS), 0) == owner).astype(F32)
    own16 = own.astype(BF16)
    upper = (
        lax.broadcasted_iota(jnp.int32, (128, 128), 0) < lax.broadcasted_iota(jnp.int32, (128, 128), 1)
    ).astype(F32).astype(BF16)
    seen = jnp.zeros((NDEV, 1), F32)
    blocks = []
    for i in range(CELLS // 128):
        part = own[:, 128 * i : 128 * (i + 1)]
        blocks.append(nn_dot(part.astype(BF16), upper) + seen)
        seen = seen + jnp.sum(part, axis=1, keepdims=True)
    before = jnp.concatenate(blocks, axis=1)
    where = jnp.sum(before * own, axis=0, keepdims=True).astype(jnp.int32)
    target = jnp.where(valid, owner * CAP + where, CELLS)
    ohs_ref[...] = (lax.broadcasted_iota(jnp.int32, (CELLS, CELLS), 0) == target).astype(F32).astype(BF16)

    wd = wd_ref[...]
    cw, sw = jnp.cos(wd), jnp.sin(wd)
    wg = wg_ref[...]
    acc = jnp.zeros((8, CELLS), F32)
    acc4 = jnp.zeros((4, CELLS), F32)
    for f in range(NF):
        if f % 5 == 0:
            loads[f // 5].wait()
        s = spec_ref[f, 0:8, :] + spec_ref[f, 8:16, :] + spec_ref[f, 16:24, :] + spec_ref[f, 24:32, :]
        acc = acc + WIDTH[f] * s
        acc4 = acc4 + WIDTH[f] * spec_ref[f, 32:36, :]
    energy = jnp.sum(acc, axis=0, keepdims=True) + jnp.sum(acc4, axis=0, keepdims=True)
    load = 0.4 * (energy / (energy + 10.0))
    for d in range(ND):
        lobe = jnp.maximum(COS[d] * cw + SIN[d] * sw, 0.0)
        r_ref[d : d + 1, :] = wg * (lobe * lobe) - load

    last_base = 36 * (NF - 1)
    v_ref[last_base : last_base + 32, :] = spec_ref[NF - 1, 0:32, :] * jnp.exp(RATIO[NF - 1] * r_ref[0:32, :])
    v_ref[last_base + 32 : last_base + 36, :] = spec_ref[NF - 1, 32:36, :] * jnp.exp(RATIO[NF - 1] * r_ref[32:36, :])

    b_ref[...] = jnp.zeros_like(b_ref)
    last = v_ref[128 * NT : 128 * NT + 4, :]
    ident = (local + 1).astype(F32)
    for s in range(CAP):
        here = (where == s).astype(F32)
        b_ref[4 * s : 4 * s + 4, :] = last * here
        b_ref[4 * CAP + s : 4 * CAP + s + 1, :] = ident * here
    bh, bl = split(b_ref[...])
    sbuf[:, 8, :] = nt_dot(own16, bh) + nt_dot(own16, bl)

    def push(rows, sem):
        pltpu.make_async_copy(sbuf.at[me, rows], rbuf.at[me, rows], sem).start()

        def go(j, carry):
            b, e, dc = lax.rem(j, 4), lax.rem(lax.div(j, 4), 4), lax.div(j, 16)
            cc = lax.rem(c + dc, 2)
            for a in range(4):
                lo = (lax.rem(y + b + a, 4) * 4 + lax.rem(z + e + a, 4)) * 2 + cc
                la = lax.rem(x + a, 4)
                copy = pltpu.make_async_remote_copy(
                    src_ref=sbuf.at[lo * NLAT + la, rows], dst_ref=rbuf.at[me, rows],
                    send_sem=send_sem, recv_sem=sem, device_id=(lo, la), device_id_type=MESH,
                )
                if a == 0:
                    pl.when(j > 0)(copy.start)
                else:
                    copy.start()
            return carry

        lax.fori_loop(0, NDEV // 4, go, 0)

    def tile(t):
        return pl.ds(pl.multiple_of(8 * (t + jnp.minimum(t, 1)), 8), 8)

    front = pl.ds(0, 9)

    def arrive(rows, sem):
        pltpu.make_async_copy(rbuf.at[:, rows], rbuf.at[:, rows], sem).wait()

    def grow(q, carry):
        base = pl.multiple_of(72 * q, 8)
        f, g = 2 * q, 2 * q + 1
        e4 = []
        for i, h in enumerate((f, g)):
            ratio = table[h]
            v_ref[pl.ds(base + 32 * i, 32), :] = spec_ref[h, 0:32, :] * jnp.exp(ratio * r_ref[0:32, :])
            e4.append(spec_ref[h, 32:36, :] * jnp.exp(ratio * r_ref[32:36, :]))
        v_ref[pl.ds(base + 64, 8), :] = jnp.concatenate(e4, axis=0)
        return carry

    def pairs(t):
        return jnp.where(t == 0, 0, jnp.minimum(lax.div(16 * t + 8, 9), NF // 2))

    def group(t):
        lax.fori_loop(pairs(t), pairs(t + 1), grow, 0)
        hi, lo = split(v_ref[pl.ds(pl.multiple_of(128 * t, 128), 128), :])
        both = nt_dot(ohs_ref[...], jnp.concatenate([hi, lo], axis=0))
        res = both[:, :128] + both[:, 128:]
        sbuf[:, tile(t), :] = res.reshape(NDEV, CAP, 128)

    group(jnp.int32(0))
    pl.semaphore_wait(barrier, NDEV - 1)
    push(front, recv_sem.at[0])

    def prologue(t, carry):
        group(t)

        @pl.when(t < 3)
        def _():
            push(tile(t), recv_sem.at[t])

        return carry

    lax.fori_loop(1, 4, prologue, 0)

    sh = as_tile(sh_ref)
    sea = as_tile(mask_ref).astype(F32)
    fill_turns(turn_ref, sx_ref, sy_ref)
    lat = Lattice()
    low = (x > 0).astype(F32)
    high = (x < NLAT - 1).astype(F32)

    arrive(front, recv_sem.at[0])
    tail = rbuf[:, 8, :]
    ident = tail[:, 4 * CAP : 5 * CAP]
    spread = (
        lax.broadcasted_iota(jnp.int32, (CAP, CELLS), 1) % CAP == lax.broadcasted_iota(jnp.int32, (CAP, CELLS), 0)
    ).astype(F32).astype(BF16)
    ih, il = split(ident)
    wide = nn_dot(ih, spread) + nn_dot(il, spread)
    mine = lax.broadcasted_iota(jnp.int32, (NDEV, CELLS), 1) // CAP == lax.broadcasted_iota(jnp.int32, (NDEV, CELLS), 0)
    ids = jnp.sum(jnp.where(mine, wide, 0.0), axis=0, keepdims=True).astype(jnp.int32) - 1
    ohr_ref[...] = (lax.broadcasted_iota(jnp.int32, (CELLS, CELLS), 0) == ids).astype(F32).astype(BF16)
    cols = []
    th, tl = split(tail)
    for k in range(4):
        pick = (
            lax.broadcasted_iota(jnp.int32, (128, CELLS), 0) == 4 * (lax.broadcasted_iota(jnp.int32, (128, CELLS), 1) % CAP) + k
        ).astype(F32).astype(BF16)
        w = nn_dot(th, pick) + nn_dot(tl, pick)
        cols.append(jnp.sum(jnp.where(mine, w, 0.0), axis=0, keepdims=True))
    ch, cl = split(jnp.concatenate(cols + [jnp.zeros((4, CELLS), F32)], axis=0))
    tailv = nt_dot(ch, ohr_ref[...]) + nt_dot(cl, ohr_ref[...])
    for ct in range(8):
        field_ref[128 * NT : 128 * NT + 8, ct, :] = tailv[:, 128 * ct : 128 * (ct + 1)]

    def unplace(t):
        hi, lo = split(rbuf[:, tile(t), :].reshape(CELLS, 128))
        both = nn_dot(ohr_ref[...], jnp.concatenate([hi, lo], axis=1))
        res = both[:, :128] + both[:, 128:]
        for ct in range(8):
            field_ref[pl.ds(pl.multiple_of(128 * t, 128), 128), ct, :] = res[128 * ct : 128 * (ct + 1), :].T

    def faces(s, f):
        bufs = zip((up_out, dn_out, yp_out, ym_out), (up_in, dn_in, yp_in, ym_in), (nxt, prv, ynxt, yprv))
        return [
            pltpu.make_async_remote_copy(
                src_ref=src.at[s, f], dst_ref=dst.at[s, f], send_sem=face_send.at[s, n],
                recv_sem=face_recv.at[s, n, f], device_id=who, device_id_type=MESH,
            )
            for n, (src, dst, who) in enumerate(bufs)
        ]

    def send(s, f):
        for copy in faces(s, f):
            copy.start()

    def await_faces(s, f):
        for copy in faces(s, f):
            copy.wait_recv()

    def outgoing(s, f):
        return Faces(lat, up_out.at[s, f], dn_out.at[s, f], yp_out.at[s, f], ym_out.at[s, f])

    def propagate(s, f, get, put):
        await_faces(s, f)
        substep(
            lat, get, sh, sea, lambda d: turn_ref[d], table[32 + f],
            lambda k: up_in[s, f, k], lambda k: dn_in[s, f, k], yp_in[s, f] * low, ym_in[s, f] * high, put,
        )

    def over(lo, hi, fn):
        def body(f, carry):
            fn(f)
            return carry

        lax.fori_loop(lo, hi, body, 0)

    def chain(lo, hi, fn, s):
        def body(f, carry):
            fn(f)

            @pl.when(f > lo)
            def _():
                send(s, f - 1)

            return carry

        lax.fori_loop(lo, hi, body, 0)

        @pl.when(hi > lo)
        def _():
            send(s, hi - 1)

    def start_face(f):
        face = outgoing(0, f)
        for d in range(ND):
            face.put(d, sh * field_ref[row_dyn(f, d)])
        face.close()

    def first(f):
        face = outgoing(1, f)

        def put(d, v):
            f1_ref[f, d] = v
            face.put(d, sh * v)

        propagate(0, f, lambda d: field_ref[row_dyn(f, d)], put)
        face.close()

    def second(f):
        def put(d, v):
            stage_ref[f, d, pl.ds(0, 4, 2), :] = v[0:4, :]
            stage_ref[f, d, pl.ds(1, 4, 2), :] = v[4:8, :]

        propagate(1, f, lambda d: f1_ref[f, d], put)

    def emit(f):
        pltpu.make_async_copy(stage_ref.at[f], out_hbm.at[f], out_sem).start()

    def step(t, carry):
        @pl.when((t > 0) & (t < NT))
        def _():
            arrive(tile(t), recv_sem.at[t])

        @pl.when(t < NT)
        def _():
            unplace(t)

        chain(whole(t), whole(t + 1), start_face, 0)

        @pl.when(t + 3 < NT)
        def _():
            push(tile(t + 3), recv_sem.at[t + 3])

        @pl.when(t + 4 < NT)
        def _():
            group(t + 4)

        chain(whole(t - 1), whole(t), first, 1)
        over(whole(t - 2), whole(t - 1), second)
        over(whole(t - 2), whole(t - 1), emit)
        return carry

    lax.fori_loop(0, NT + 2, step, 0)
    sent = sbuf.at[pl.ds(0, NDEV - 1), pl.ds(0, ROWS)]
    pltpu.make_async_copy(sent, sent, send_sem).wait()
    for s in range(2):
        for n, src in enumerate((up_out, dn_out, yp_out, ym_out)):
            pltpu.make_async_copy(src.at[s], src.at[s], face_send.at[s, n]).wait()
    pltpu.make_async_copy(stage_ref, out_hbm, out_sem).wait()


def emit_kernel(in_ref, out_ref, buf, in_sem, out_sem):
    def part(i):
        return pl.ds(5 * i, 5)

    reads = [pltpu.make_async_copy(in_ref.at[part(i)], buf.at[part(i)], in_sem.at[i]) for i in range(5)]
    writes = [pltpu.make_async_copy(buf.at[part(i)], out_ref.at[part(i)], out_sem.at[i]) for i in range(5)]
    for cp in reads:
        cp.start()
    for read, write in zip(reads, writes):
        read.wait()
        write.start()
    for cp in writes:
        cp.wait()


def on_device(spectra, wind_growth, wind_dir, point_cell, land_mask, shoaling, slope_x, slope_y):
    face = [(2, NF, PHALF, 8, 128), (2, NF, PHALF, 8, 128), (2, NF, 8, 128), (2, NF, 8, 128)]
    out = pl.pallas_call(
        step_kernel,
        out_shape=jax.ShapeDtypeStruct((NF, ND, 8, 128), F32),
        in_specs=[pl.BlockSpec(memory_space=pl.ANY)] * 8,
        out_specs=pl.BlockSpec(memory_space=pl.ANY),
        scratch_shapes=[
            pltpu.VMEM((1, CELLS), F32),
            pltpu.VMEM((1, CELLS), F32),
            pltpu.VMEM((1, CELLS), jnp.int32),
            pltpu.VMEM((GX, GY), jnp.int32),
            pltpu.VMEM((GX, GY), F32),
            pltpu.VMEM((GX, GY), F32),
            pltpu.VMEM((GX, GY), F32),
            pltpu.VMEM((NF, ND, CELLS), F32),
            pltpu.VMEM((40, CELLS), F32),
            pltpu.VMEM((904, CELLS), F32),
            pltpu.VMEM((128, CELLS), F32),
            pltpu.VMEM((NDEV, 64, 128), F32),
            pltpu.VMEM((NDEV, 64, 128), F32),
            pltpu.VMEM((CELLS, CELLS), BF16),
            pltpu.VMEM((CELLS, CELLS), BF16),
            pltpu.VMEM((904, 8, 128), F32),
            pltpu.VMEM((NF, ND, 8, 128), F32),
            pltpu.VMEM((NF, ND, 8, 128), F32),
            pltpu.VMEM((ND, 8, 128), F32),
        ]
        + [pltpu.VMEM(s, F32) for s in face] * 2
        + [
            pltpu.SMEM((64,), F32),
            pltpu.SemaphoreType.DMA((7,)),
            pltpu.SemaphoreType.DMA((5,)),
            pltpu.SemaphoreType.DMA,
            pltpu.SemaphoreType.DMA((NT,)),
            pltpu.SemaphoreType.DMA((2, 4)),
            pltpu.SemaphoreType.DMA((2, 4, NF)),
            pltpu.SemaphoreType.DMA,
        ],
        compiler_params=pltpu.CompilerParams(collective_id=0, has_side_effects=True, vmem_limit_bytes=VMEM_LIMIT),
        name="wave_step",
    )(
        spectra, wind_growth.reshape(1, CELLS), wind_dir.reshape(1, CELLS), point_cell.reshape(1, CELLS),
        land_mask, shoaling, slope_x, slope_y,
    )
    out = pl.pallas_call(
        emit_kernel,
        out_shape=jax.ShapeDtypeStruct((NF, ND, 8, 128), F32),
        in_specs=[pl.BlockSpec(memory_space=pl.ANY)],
        out_specs=pl.BlockSpec(memory_space=pl.ANY),
        scratch_shapes=[
            pltpu.VMEM((NF, ND, 8, 128), F32),
            pltpu.SemaphoreType.DMA((5,)),
            pltpu.SemaphoreType.DMA((5,)),
        ],
        compiler_params=pltpu.CompilerParams(vmem_limit_bytes=VMEM_LIMIT),
        name="emit",
    )(out)
    out = out.reshape(NF, ND, 4, GX, 128)
    return jnp.transpose(out, (0, 1, 3, 2, 4)).reshape(NF, ND, GX, GY)


def solution(mesh):
    placed = (
        P(None, None, ("lon", "lat")),
        P(("lon", "lat")),
        P(("lon", "lat")),
        P(("lon", "lat")),
        P("lon", "lat"),
        P("lon", "lat"),
        P("lon", "lat"),
        P("lon", "lat"),
    )
    return jax.shard_map(
        on_device, mesh=mesh, in_specs=placed, out_specs=P(None, None, "lon", "lat"), check_vma=False
    )
```
